768 devices in a mesh: dp: 24 (over z_hi, y), frame: 8 (over z_lo, core), mp: 4 (over x).
Axes of the slice: x: 4, y: 8, z: 12 (z_hi: 3, z_lo: 4; z = z_hi * 4 + z_lo), core: 2. Of those that a mesh axis runs over, the one named last changes fastest.
Arguments:
- projected: bfloat16 [6, 24, 16, 128, 5120], P(None, 'dp', 'frame', None, 'mp'), may hold values from -6 to 6
- codes: float32 [24, 16, 32], P('dp'), may hold values from -6 to 6
- action_weight: float32 [32, 5120], P(None, 'mp'), may hold values from -1 to 1
- clip_ids: int32 [24], replicated, may hold values from 0 to 23, each once
- frame_map: int32 [16], replicated, may hold values from 0 to 15, each once
- segments: int32 [24, 16], P('dp'), may hold values from 0 to 2, never falling along the last dimension, each value on 1 to 8 neighbouring positions
Outputs:
- mixed: bfloat16 [24, 16, 128, 5120], P('dp', 'frame', None, 'mp')
The draws below stay inside these ranges and needn't reach their ends.
Inputs may be any that keep to these rules, and one draw needn't show every extreme that they name: `clip_ids`: each clip id appears once. `frame_map`: each time appears once. `segments`: episode numbers never fall along time.
All inputs are finite; a program needn't handle non-finite values.
Results may differ from the reference program's by a relative error of at most 0.0085.
Values may be sent and summed in bfloat16 or wider, within the bound.
A program may use at most 32 MiB of HBM per device.

```python
import math
import jax
import jax.numpy as jnp
import numpy as np
from jax import lax

D = 5120
E = 128
F = 16
A = 32
P_SIZE = 128
CLIPS = 24


def draw_projected(key, part):
    key_base = jax.random.fold_in(key, 0)
    shape = (6, CLIPS, F, P_SIZE, D)
    base = jax.random.normal(key_base, shape, jnp.float32)
    spread = jnp.array([1.6, 1.6, 1.0, 1.6, 1.6, 1.0], jnp.float32).reshape(6, 1, 1, 1, 1)
    base = jnp.clip(base * spread, -6.0, 6.0)
    return base.astype(jnp.bfloat16)


def shard_levels(own_key, dims, pieces, least, largest):
    def one(axis_at, shards_of):
        heights = jax.random.uniform(jax.random.fold_in(jax.random.fold_in(own_key, 6), axis_at), (shards_of,), jnp.float32, least / len(pieces), largest / len(pieces))
        return jnp.repeat(jnp.exp(heights), dims[axis_at] // shards_of).reshape((-1,) + (1,) * (len(dims) - axis_at - 1))

    loudness = one(*pieces[0])
    for cut in pieces[1:]:
        loudness = loudness * one(*cut)
    return loudness


def length_profile(amount, total, reach, lean):
    portions = [(1 << 20) // math.isqrt(grade ** lean) + 1 for grade in range(2, amount + 1)]
    surplus, given = total - reach - (amount - 1), [1] * (amount - 1)
    while surplus > 0:
        movable = [i for i in range(amount - 1) if given[i] < reach]
        whole, remaining = sum([portions[i] for i in movable]), surplus
        for i in movable:
            extra = min(reach - given[i], max(1, remaining * portions[i] // whole), surplus)
            given[i] = given[i] + extra
            surplus = surplus - extra
    return np.array([reach] + given)


def ragged_sizes(own_key, amount, total, reach, skew):
    if amount == 2:
        one = jax.random.randint(own_key, (), max(1, total - reach), min(reach, total - 1) + 1)
        return jnp.stack([one, total - one])
    lengths = jnp.asarray(length_profile(amount, total, reach, skew), jnp.int32)
    twos = (amount - 1) // 2
    source_of, sink = lengths[1:1 + 2 * twos:2], lengths[2:2 + 2 * twos:2]
    slack = jnp.minimum(source_of - 1, reach - sink)
    shifted = jax.random.randint(jax.random.fold_in(own_key, 1), (twos,), 0, 1 << 20) % (slack + 1)
    lengths = lengths.at[1:1 + 2 * twos:2].set(source_of - shifted).at[2:2 + 2 * twos:2].set(sink + shifted)
    return lengths[jax.random.permutation(jax.random.fold_in(own_key, 2), amount)]


def gaussian(key, shape, scale, limit, shards=(), kind=jnp.bfloat16):
    gain = shard_levels(key, shape, shards, -0.22, 0.18) if shards else 1.0
    values = jax.random.normal(key, shape, jnp.float32) * scale * gain
    return jnp.minimum(jnp.maximum(values, -limit), limit).astype(kind)


def setup_inputs(seed: int = 0) -> dict:
    splits = jax.random.split(jax.random.key(seed), 7)
    return {
        "projected": draw_projected(jax.random.fold_in(splits[6], 71), 0),
        "codes": gaussian(splits[1], (CLIPS, F, A), 1.0, 6.0, ((0, 24),), jnp.float32),
        "action_weight": gaussian(splits[2], (A, D), A ** -0.5, 1.0, ((1, 4),), jnp.float32),
        "clip_ids": jax.random.permutation(splits[3], CLIPS).astype(jnp.int32),
        "frame_map": jax.random.permutation(splits[4], F).astype(jnp.int32),
        "segments": jax.vmap(lambda own: jnp.searchsorted(jnp.cumsum(ragged_sizes(own, 3, F, 8, 0)), jnp.arange(F), side="right"))(jax.random.split(splits[5], CLIPS)).reshape((CLIPS, F)).astype(jnp.int32),
    }


def masked_softmax(spatial_scores, allowed):
    peak = jnp.max(jnp.where(allowed, spatial_scores, -1e30), axis=-1, keepdims=True)
    weights = jnp.where(allowed, jnp.exp(spatial_scores - peak), 0.0)
    return (weights / jnp.sum(weights, axis=-1, keepdims=True)).astype(jnp.bfloat16)


def reference(projected, codes, action_weight, clip_ids, frame_map, segments):
    heads = D // E
    reshaped_rows = projected.reshape(6, CLIPS, F, P_SIZE, heads, E)
    score_scale = 1.0 / (E ** 0.5)
    head_patches = lax.Precision.HIGHEST
    select = (clip_ids[:, None] == jnp.arange(CLIPS, dtype=jnp.int32)[None, :]).astype(jnp.float32)
    by_clip = jnp.einsum('ic,ifa->cfa', select, codes, precision=head_patches)
    action = jnp.einsum('cfa,ad->cfd', by_clip, action_weight, precision=head_patches)
    action_slot = action[:, frame_map]
    values = (reshaped_rows[5].astype(jnp.float32) + action_slot.reshape(CLIPS, F, 1, heads, E)).astype(jnp.bfloat16)
    seg_slot = segments[:, frame_map]
    allowed = (frame_map[None, :] <= frame_map[:, None])[None] & (seg_slot[:, None, :] == seg_slot[:, :, None])

    def per_clip(token_index):
        spatial_query = reshaped_rows[0, token_index].astype(jnp.float32)
        spatial_key = reshaped_rows[1, token_index].astype(jnp.float32)
        svalue = reshaped_rows[2, token_index].astype(jnp.float32)
        spatial_scores = jnp.einsum('bjvo,bcvo->bvjc', spatial_query, spatial_key, precision=head_patches) * score_scale
        probs = masked_softmax(spatial_scores, jnp.ones(spatial_scores.shape, bool))
        spatial = jnp.einsum('fhpq,fqhe->fphe', probs.astype(jnp.float32), svalue, precision=head_patches).astype(jnp.bfloat16)
        tquery = reshaped_rows[3, token_index].astype(jnp.float32)
        tkey = reshaped_rows[4, token_index].astype(jnp.float32)
        tvalue = values[token_index].astype(jnp.float32)
        tscores = jnp.einsum('sphe,tphe->phst', tquery, tkey, precision=head_patches) * score_scale
        tprobs = masked_softmax(tscores, allowed[token_index][None, None])
        temporal = jnp.einsum('phst,tphe->sphe', tprobs.astype(jnp.float32), tvalue, precision=head_patches).astype(jnp.bfloat16)
        return (spatial.astype(jnp.float32) + temporal.astype(jnp.float32)).astype(jnp.bfloat16)

    mixed = lax.map(per_clip, jnp.arange(CLIPS, dtype=jnp.int32))
    return mixed.reshape(CLIPS, F, P_SIZE, D)
```

```python
import functools

import jax
import jax.numpy as jnp
from jax import lax
from jax.experimental import pallas as pl
from jax.experimental.pallas import tpu as pltpu
from jax.sharding import PartitionSpec as P

MESH = pl.DeviceIdType.MESH
E = 128
FAR = 3
HEADS = 2


def softmax(scores):
    peak = jnp.max(scores, axis=-1, keepdims=True)
    weights = jnp.exp(scores - peak)
    return (weights / jnp.sum(weights, axis=-1, keepdims=True)).astype(jnp.bfloat16)


def scores_of(q, k):
    return lax.dot_general(
        q, k, (((1,), (1,)), ((), ())), preferred_element_type=jnp.float32
    )


def kernel(
    sizes,
    clip_ids,
    frame_map,
    segments,
    codes,
    weight,
    projected,
    out,
    far_codes,
    all_codes,
    action,
    bias,
    own,
    spatial,
    got,
    done,
    back,
    result,
    far_send,
    far_recv,
    near_send,
    near_recv,
    code_sem,
    own_sem,
    send_sem,
    recv_sem,
    back_send,
    back_recv,
    out_sem,
):
    clips, group, frames, patches, width = sizes
    near = clips // FAR
    share = patches // group
    slots = group * frames
    rows = slots * share
    wide = HEADS * E
    chunks = width // wide
    scale = 1.0 / E**0.5
    clip = lax.axis_index("dp")
    me = lax.axis_index("frame")
    mp = lax.axis_index("mp")
    my_far, my_near = clip // near, lax.rem(clip, near)
    core = lax.rem(me, 2)

    def far_peer(j):
        return lax.rem(my_far + j, FAR)

    def near_peer(j):
        return lax.rem(my_near + j, near)

    def peer_of(j):
        step = jnp.where(core == 0, j, group - j)
        return jnp.bitwise_xor(me, step)

    barrier = pltpu.get_barrier_semaphore()
    for j in range(1, group):
        pl.semaphore_signal(
            barrier, inc=1, device_id=(clip, peer_of(j), mp), device_id_type=MESH
        )
    for j in range(1, FAR):
        pl.semaphore_signal(
            barrier,
            inc=1,
            device_id=(far_peer(j) * near + my_near, me, mp),
            device_id_type=MESH,
        )
    for j in range(1, near):
        pl.semaphore_signal(
            barrier,
            inc=1,
            device_id=(my_far * near + near_peer(j), me, mp),
            device_id_type=MESH,
        )

    own_code = pltpu.make_async_copy(codes.at[0], far_codes.at[my_far], code_sem.at[0])
    own_code.start()
    own_in = pltpu.make_async_copy(projected.at[0:3, 0], own, own_sem)
    own_in.start()
    pl.semaphore_wait(barrier, group - 1 + FAR - 1 + near - 1)

    def far_copy(j):
        return pltpu.make_async_remote_copy(
            src_ref=codes.at[0],
            dst_ref=far_codes.at[my_far],
            send_sem=far_send.at[j],
            recv_sem=far_recv.at[j],
            device_id=(far_peer(j) * near + my_near, me, mp),
            device_id_type=MESH,
        )

    for j in range(1, FAR):
        far_copy(j).start()

    def part(ref, owner, chunk):
        columns = pl.ds(pl.multiple_of(chunk * wide, wide), wide)
        rows_of = pl.ds(pl.multiple_of(owner * share, share), share)
        return ref.at[3:6, 0, :, rows_of, columns]

    def exchange(chunk, j):
        peer = peer_of(j)
        return pltpu.make_async_remote_copy(
            src_ref=part(projected, peer, chunk),
            dst_ref=got.at[chunk, me],
            send_sem=send_sem.at[chunk, j],
            recv_sem=recv_sem.at[chunk, j],
            device_id=(clip, peer, mp),
            device_id_type=MESH,
        )

    def keep(chunk):
        return pltpu.make_async_copy(
            part(projected, me, chunk), got.at[chunk, me], recv_sem.at[chunk, 0]
        )

    def start_chunk(chunk, carry):
        for j in range(1, group):
            exchange(chunk, j).start()
        keep(chunk).start()
        return carry

    lax.fori_loop(0, chunks, start_chunk, 0)

    for j in range(1, FAR):
        far_copy(j).wait_recv()
    own_code.wait()

    def near_copy(j):
        return pltpu.make_async_remote_copy(
            src_ref=far_codes,
            dst_ref=all_codes.at[my_near],
            send_sem=near_send.at[j],
            recv_sem=near_recv.at[j],
            device_id=(my_far * near + near_peer(j), me, mp),
            device_id_type=MESH,
        )

    for j in range(1, near):
        near_copy(j).start()
    near_own = pltpu.make_async_copy(far_codes, all_codes.at[my_near], code_sem.at[1])
    near_own.start()

    row = lax.broadcasted_iota(jnp.int32, (rows, rows), 0)
    column = lax.broadcasted_iota(jnp.int32, (rows, rows), 1)
    row_time = jnp.zeros((rows, 1), jnp.int32)
    row_part = jnp.zeros((rows, 1), jnp.int32)
    col_time = jnp.zeros((1, rows), jnp.int32)
    col_part = jnp.zeros((1, rows), jnp.int32)
    row_slot = lax.broadcasted_iota(jnp.int32, (rows, 1), 0) // share
    col_slot = lax.broadcasted_iota(jnp.int32, (1, rows), 1) // share
    for s in range(slots):
        time = frame_map[s]
        episode = segments[0, time]
        row_time = jnp.where(row_slot == s, time, row_time)
        row_part = jnp.where(row_slot == s, episode, row_part)
        col_time = jnp.where(col_slot == s, time, col_time)
        col_part = jnp.where(col_slot == s, episode, col_part)
    allowed = (
        (lax.rem(row, share) == lax.rem(column, share))
        & (col_time <= row_time)
        & (col_part == row_part)
    )
    bias[...] = jnp.where(allowed, 0.0, -1e30)

    own_in.wait()

    def one_head(head, carry):
        lanes = pl.ds(pl.multiple_of(head * E, E), E)
        for f in range(frames):
            probs = softmax(scores_of(own[0, f, :, lanes], own[1, f, :, lanes]) * scale)
            spatial[f, :, lanes] = jnp.dot(
                probs, own[2, f, :, lanes], preferred_element_type=jnp.float32
            ).astype(jnp.bfloat16)
        return carry

    lax.fori_loop(0, width // E, one_head, 0)

    for j in range(1, near):
        near_copy(j).wait_recv()
    near_own.wait()
    by_clip = jnp.zeros(codes.shape[1:], jnp.float32)
    for i in range(clips):
        by_clip = by_clip + jnp.where(
            clip_ids[i] == clip, all_codes[i % near, i // near], 0.0
        )
    slot_of = lax.broadcasted_iota(jnp.int32, (slots, 1), 0)
    time_of = jnp.zeros((slots, 1), jnp.int32)
    for s in range(slots):
        time_of = jnp.where(slot_of == s, frame_map[s], time_of)
    by_slot = jnp.zeros(by_clip.shape, jnp.float32)
    for t in range(slots):
        by_slot = by_slot + jnp.where(time_of == t, by_clip[t : t + 1], 0.0)
    action[...] = jnp.dot(
        by_slot,
        weight[...],
        precision=lax.Precision.HIGHEST,
        preferred_element_type=jnp.float32,
    )

    def give(chunk, j):
        peer = peer_of(j)
        return pltpu.make_async_remote_copy(
            src_ref=done.at[chunk, peer],
            dst_ref=back.at[chunk, me],
            send_sem=back_send.at[chunk, j],
            recv_sem=back_recv.at[chunk, j],
            device_id=(clip, peer, mp),
            device_id_type=MESH,
        )

    def give_self(chunk):
        return pltpu.make_async_copy(
            done.at[chunk, me], back.at[chunk, me], back_recv.at[chunk, 0]
        )

    def attend(chunk, carry):
        for j in range(1, group):
            exchange(chunk, j).wait_recv()
        keep(chunk).wait()
        for h in range(HEADS):
            lanes = slice(h * E, (h + 1) * E)
            q = got[chunk, :, 0, :, :, lanes].reshape(rows, E)
            k = got[chunk, :, 1, :, :, lanes].reshape(rows, E)
            raw = got[chunk, :, 2, :, :, lanes].reshape(slots, share, E)
            added = action[:, pl.ds(pl.multiple_of(chunk * wide + h * E, E), E)]
            v = (raw.astype(jnp.float32) + added[:, None, :]).astype(jnp.bfloat16)
            probs = softmax(scores_of(q, k) * scale + bias[...])
            mixed = jnp.dot(
                probs, v.reshape(rows, E), preferred_element_type=jnp.float32
            ).astype(jnp.bfloat16)
            done[chunk, :, :, :, lanes] = mixed.reshape(group, frames, share, E)
        for j in range(1, group):
            give(chunk, j).start()
        give_self(chunk).start()
        return carry

    lax.fori_loop(0, chunks, attend, 0)

    def write(chunk):
        columns = pl.ds(pl.multiple_of(chunk * wide, wide), wide)
        return pltpu.make_async_copy(
            result.at[chunk], out.at[0, :, :, columns], out_sem.at[chunk]
        )

    def finish(chunk, carry):
        for j in range(1, group):
            give(chunk, j).wait_recv()
        give_self(chunk).wait()
        columns = pl.ds(pl.multiple_of(chunk * wide, wide), wide)
        for f in range(frames):
            temporal = back[chunk, :, f].reshape(patches, wide).astype(jnp.float32)
            result[chunk, f] = (
                spatial[f, :, columns].astype(jnp.float32) + temporal
            ).astype(jnp.bfloat16)
        write(chunk).start()
        return carry

    lax.fori_loop(0, chunks, finish, 0)

    def drain(chunk, carry):
        for j in range(1, group):
            exchange(chunk, j).wait_send()
            give(chunk, j).wait_send()
        write(chunk).wait()
        return carry

    lax.fori_loop(0, chunks, drain, 0)
    for j in range(1, FAR):
        far_copy(j).wait_send()
    for j in range(1, near):
        near_copy(j).wait_send()


def solution(mesh):
    clips, group = mesh.shape["dp"], mesh.shape["frame"]

    def local(projected, codes, weight, clip_ids, frame_map, segments):
        _, _, frames, patches, width = projected.shape
        near = clips // FAR
        share = patches // group
        slots = group * frames
        rows = slots * share
        wide = HEADS * E
        chunks = width // wide
        smem = pl.BlockSpec(memory_space=pltpu.SMEM)
        vmem = pl.BlockSpec(memory_space=pltpu.VMEM)
        dma = pltpu.SemaphoreType.DMA
        bf16, f32 = jnp.bfloat16, jnp.float32
        return pl.pallas_call(
            functools.partial(kernel, (clips, group, frames, patches, width)),
            out_shape=jax.ShapeDtypeStruct((1, frames, patches, width), bf16),
            in_specs=[smem, smem, smem, vmem, vmem, pl.BlockSpec(memory_space=pl.ANY)],
            out_specs=pl.BlockSpec(memory_space=pl.ANY),
            scratch_shapes=[
                pltpu.VMEM((FAR, *codes.shape[1:]), f32),
                pltpu.VMEM((near, FAR, *codes.shape[1:]), f32),
                pltpu.VMEM((slots, width), f32),
                pltpu.VMEM((rows, rows), f32),
                pltpu.VMEM((3, frames, patches, width), bf16),
                pltpu.VMEM((frames, patches, width), bf16),
                pltpu.VMEM((chunks, group, 3, frames, share, wide), bf16),
                pltpu.VMEM((chunks, group, frames, share, wide), bf16),
                pltpu.VMEM((chunks, group, frames, share, wide), bf16),
                pltpu.VMEM((chunks, frames, patches, wide), bf16),
                dma((FAR,)),
                dma((FAR,)),
                dma((near,)),
                dma((near,)),
                dma((2,)),
                dma(()),
                dma((chunks, group)),
                dma((chunks, group)),
                dma((chunks, group)),
                dma((chunks, group)),
                dma((chunks,)),
            ],
            compiler_params=pltpu.CompilerParams(
                collective_id=0,
                has_side_effects=True,
                vmem_limit_bytes=67_043_328,
            ),
        )(clip_ids, frame_map, segments, codes, weight, projected)

    return jax.shard_map(
        local,
        mesh=mesh,
        in_specs=(
            P(None, "dp", "frame", None, "mp"),
            P("dp", None, None),
            P(None, "mp"),
            P(),
            P(),
            P("dp", None),
        ),
        out_specs=P("dp", "frame", None, "mp"),
        check_vma=False,
    )
```

```python
import functools

import jax
import jax.numpy as jnp
from jax import lax
from jax.experimental import pallas as pl
from jax.experimental.pallas import tpu as pltpu
from jax.sharding import PartitionSpec as P

MESH = pl.DeviceIdType.MESH
E = 128
FAR = 3
CORES = 2
SIZES = (5, 3, 2)
MOVES = 4


def softmax(scores):
    peak = jnp.max(scores, axis=-1, keepdims=True)
    weights = jnp.exp(scores - peak)
    return (weights / jnp.sum(weights, axis=-1, keepdims=True)).astype(jnp.bfloat16)


def scores_of(q, k):
    return lax.dot_general(
        q, k, (((1,), (1,)), ((), ())), preferred_element_type=jnp.float32
    )


def kernel(
    sizes,
    clip_ids_in,
    frame_map_in,
    segments_in,
    codes_in,
    weight_in,
    projected,
    out,
    clip_ids,
    frame_map,
    segments,
    codes,
    weight,
    far_codes,
    all_codes,
    action,
    bias,
    own,
    got,
    done,
    back,
    result,
    out_sem,
    small_sem,
    far_send,
    far_recv,
    far_hello,
    hello,
    near_hello,
    near_send,
    near_recv,
    code_sem,
    own_sem,
    send_sem,
    recv_sem,
    back_send,
    back_recv,
):
    clips, group, frames, patches, width = sizes
    near = clips // FAR
    share = patches // group
    slots = group * frames
    rows = slots * share
    chunks = len(SIZES)
    chips = group // CORES
    starts = [sum(SIZES[:c]) for c in range(chunks)]
    scale = 1.0 / E**0.5
    clip = lax.axis_index("dp")
    me = lax.axis_index("frame")
    mp = lax.axis_index("mp")
    my_far, my_near = clip // near, lax.rem(clip, near)
    chip, core = me // CORES, lax.rem(me, CORES)

    def peer_of(j):
        return jnp.bitwise_xor(me, j)

    def at_frame(peer):
        return (clip, peer, mp)

    def at_near(peer):
        return (my_far * near + peer, me, mp)

    def at_far(part, chip_there):
        return (part * near + my_near, chip_there * CORES + core, mp)

    ends = (chips - 1, 0)
    there = (lax.rem(my_far + 1, FAR), lax.rem(my_far + FAR - 1, FAR))

    small = [
        pltpu.make_async_copy(a, b, small_sem.at[i])
        for i, (a, b) in enumerate(
            (
                (clip_ids_in, clip_ids),
                (frame_map_in, frame_map),
                (segments_in, segments),
                (codes_in, codes),
                (weight_in, weight),
            )
        )
    ]
    own_in = pltpu.make_async_copy(projected.at[0:3, 0], own, own_sem)

    barrier = pltpu.get_barrier_semaphore()
    for peer in range(1, group):
        @pl.when(peer > me)
        def _():
            pl.semaphore_signal(
                barrier, inc=1, device_id=at_frame(peer), device_id_type=MESH
            )

    for peer in range(1, near):
        @pl.when(peer > my_near)
        def _():
            pl.semaphore_signal(
                barrier, inc=1, device_id=at_near(peer), device_id_type=MESH
            )

    for side in range(2):
        @pl.when((chip == ends[side]) & (there[side] > my_far))
        def _():
            for z in range(chips):
                pl.semaphore_signal(
                    barrier,
                    inc=1,
                    device_id=at_far(there[side], z),
                    device_id_type=MESH,
                )

        @pl.when(there[side] > my_far)
        def _():
            pl.semaphore_signal(
                barrier,
                inc=1,
                device_id=at_far(there[side], ends[1 - side]),
                device_id_type=MESH,
            )

    for copy in small:
        copy.start()
    own_in.start()
    heard = me + my_near
    for side in range(2):
        earlier = there[side] < my_far
        heard = heard + jnp.where(earlier, 1, 0)
        heard = heard + jnp.where(earlier & (chip == ends[side]), chips, 0)

    @pl.when(heard > 0)
    def _():
        pl.semaphore_wait(barrier, heard)


    def lanes_of(chunk):
        return slice(starts[chunk] * E, (starts[chunk] + SIZES[chunk]) * E)

    def part(owner, chunk):
        mine = pl.ds(pl.multiple_of(owner * share, share), share)
        return projected.at[3:6, 0, :, mine, lanes_of(chunk)]

    def exchange(chunk, peer):
        return pltpu.make_async_remote_copy(
            src_ref=part(peer, chunk),
            dst_ref=got.at[me, :, :, :, lanes_of(chunk)],
            send_sem=send_sem.at[chunk, peer],
            recv_sem=recv_sem.at[chunk, me],
            device_id=at_frame(peer),
            device_id_type=MESH,
        )

    def got_from(chunk, peer):
        return pltpu.make_async_remote_copy(
            src_ref=part(peer, chunk),
            dst_ref=got.at[peer, :, :, :, lanes_of(chunk)],
            send_sem=send_sem.at[chunk, peer],
            recv_sem=recv_sem.at[chunk, peer],
            device_id=at_frame(peer),
            device_id_type=MESH,
        )

    def keep(chunk):
        return pltpu.make_async_copy(
            part(me, chunk),
            got.at[me, :, :, :, lanes_of(chunk)],
            recv_sem.at[chunk, me],
        )

    for j in range(1, group):
        @pl.when(peer_of(j) < me)
        def _():
            exchange(0, peer_of(j)).start()
            pl.semaphore_signal(
                hello.at[me], inc=1, device_id=at_frame(peer_of(j)), device_id_type=MESH
            )

    for peer in range(1, group):
        @pl.when(peer > me)
        def _():
            pl.semaphore_wait(hello.at[peer], 1)
            exchange(0, peer).start()

    keep(0).start()
    for chunk in range(1, chunks):
        for j in range(1, group):
            exchange(chunk, peer_of(j)).start()
        keep(chunk).start()

    for peer in range(near - 1):
        @pl.when(peer < my_near)
        def _():
            pl.semaphore_signal(
                near_hello.at[my_near],
                inc=1,
                device_id=at_near(peer),
                device_id_type=MESH,
            )

    for side in range(2):
        @pl.when(there[side] < my_far)
        def _():
            pl.semaphore_signal(
                far_hello,
                inc=1,
                device_id=at_far(there[side], ends[1 - side]),
                device_id_type=MESH,
            )

    for copy in small:
        copy.wait()

    def far_copy(side, z):
        return pltpu.make_async_remote_copy(
            src_ref=codes.at[0],
            dst_ref=far_codes.at[my_far],
            send_sem=far_send.at[side, z],
            recv_sem=far_recv.at[side],
            device_id=at_far(there[side], z),
            device_id_type=MESH,
        )

    def far_start(side, when):
        @pl.when((chip == ends[side]) & when)
        def _():
            for z in range(chips):
                far_copy(side, z).start()

    for side in range(2):
        far_start(side, there[side] < my_far)
    own_code = pltpu.make_async_copy(codes.at[0], far_codes.at[my_far], code_sem.at[0])
    own_code.start()

    row = lax.broadcasted_iota(jnp.int32, (rows, rows), 0)
    column = lax.broadcasted_iota(jnp.int32, (rows, rows), 1)
    row_time = jnp.zeros((rows, 1), jnp.int32)
    row_part = jnp.zeros((rows, 1), jnp.int32)
    col_time = jnp.zeros((1, rows), jnp.int32)
    col_part = jnp.zeros((1, rows), jnp.int32)
    row_slot = lax.broadcasted_iota(jnp.int32, (rows, 1), 0) // share
    col_slot = lax.broadcasted_iota(jnp.int32, (1, rows), 1) // share
    for s in range(slots):
        time = frame_map[s]
        episode = segments[0, time]
        row_time = jnp.where(row_slot == s, time, row_time)
        row_part = jnp.where(row_slot == s, episode, row_part)
        col_time = jnp.where(col_slot == s, time, col_time)
        col_part = jnp.where(col_slot == s, episode, col_part)
    allowed = (
        (lax.rem(row, share) == lax.rem(column, share))
        & (col_time <= row_time)
        & (col_part == row_part)
    )
    bias[...] = jnp.where(allowed, 0.0, -1e30)

    own_in.wait()

    def one_head(head, carry):
        lanes = pl.ds(pl.multiple_of(head * E, E), E)
        for f in range(frames):
            probs = softmax(scores_of(own[0, f, :, lanes], own[1, f, :, lanes]) * scale)
            result[f, :, lanes] = jnp.dot(
                probs, own[2, f, :, lanes], preferred_element_type=jnp.float32
            ).astype(jnp.bfloat16)
        return carry

    lax.fori_loop(0, width // E, one_head, 0)

    for side in range(2):
        @pl.when((chip == ends[side]) & (there[side] > my_far))
        def _():
            pl.semaphore_wait(far_hello, chips)

        far_start(side, there[side] > my_far)
    own_code.wait()
    for side in range(2):
        pltpu.make_async_remote_copy(
            src_ref=codes.at[0],
            dst_ref=far_codes.at[there[1 - side]],
            send_sem=far_send.at[side, 0],
            recv_sem=far_recv.at[side],
            device_id=at_far(there[side], 0),
            device_id_type=MESH,
        ).wait_recv()

    def near_copy(peer, source):
        return pltpu.make_async_remote_copy(
            src_ref=far_codes,
            dst_ref=all_codes.at[source],
            send_sem=near_send.at[peer],
            recv_sem=near_recv.at[source],
            device_id=at_near(peer),
            device_id_type=MESH,
        )

    for peer in range(near):
        @pl.when(peer < my_near)
        def _():
            near_copy(peer, my_near).start()

    for peer in range(near):
        @pl.when(peer > my_near)
        def _():
            pl.semaphore_wait(near_hello.at[peer], 1)
            near_copy(peer, my_near).start()

    near_own = pltpu.make_async_copy(far_codes, all_codes.at[my_near], code_sem.at[1])
    near_own.start()
    for peer in range(near):
        @pl.when(peer != my_near)
        def _():
            near_copy(peer, peer).wait_recv()

    near_own.wait()

    by_clip = jnp.zeros(codes.shape[1:], jnp.float32)
    for i in range(clips):
        by_clip = by_clip + jnp.where(
            clip_ids[i] == clip, all_codes[i % near, i // near], 0.0
        )
    slot_of = lax.broadcasted_iota(jnp.int32, (slots, 1), 0)
    time_of = jnp.zeros((slots, 1), jnp.int32)
    for s in range(slots):
        time_of = jnp.where(slot_of == s, frame_map[s], time_of)
    by_slot = jnp.zeros(by_clip.shape, jnp.float32)
    for t in range(slots):
        by_slot = by_slot + jnp.where(time_of == t, by_clip[t : t + 1], 0.0)
    action[...] = jnp.dot(
        by_slot,
        weight[...],
        precision=lax.Precision.HIGHEST,
        preferred_element_type=jnp.float32,
    )

    def give(chunk, j):
        peer = peer_of(j)
        return pltpu.make_async_remote_copy(
            src_ref=done.at[peer, :, :, lanes_of(chunk)],
            dst_ref=back.at[me, :, :, lanes_of(chunk)],
            send_sem=back_send.at[chunk, j],
            recv_sem=back_recv.at[chunk, j],
            device_id=at_frame(peer),
            device_id_type=MESH,
        )

    def give_self(chunk):
        return pltpu.make_async_copy(
            done.at[me, :, :, lanes_of(chunk)],
            back.at[me, :, :, lanes_of(chunk)],
            back_recv.at[chunk, 0],
        )

    def attend(head, carry):
        lanes = pl.ds(pl.multiple_of(head * E, E), E)
        q = got[:, 0, :, :, lanes].reshape(rows, E)
        k = got[:, 1, :, :, lanes].reshape(rows, E)
        raw = got[:, 2, :, :, lanes].reshape(slots, share, E)
        added = action[:, lanes]
        v = (raw.astype(jnp.float32) + added[:, None, :]).astype(jnp.bfloat16)
        probs = softmax(scores_of(q, k) * scale + bias[...])
        mixed = jnp.dot(
            probs, v.reshape(rows, E), preferred_element_type=jnp.float32
        ).astype(jnp.bfloat16)
        done[:, :, :, lanes] = mixed.reshape(group, frames, share, E)
        return carry

    for chunk in range(chunks):
        for j in range(1, group):
            got_from(chunk, peer_of(j)).wait_recv()
        keep(chunk).wait()
        lax.fori_loop(starts[chunk], starts[chunk] + SIZES[chunk], attend, 0)
        for j in range(1, group):
            give(chunk, j).start()
        give_self(chunk).start()

    def write(chunk):
        lanes = lanes_of(chunk)
        return pltpu.make_async_copy(
            result.at[:, :, lanes], out.at[0, :, :, lanes], out_sem.at[chunk]
        )

    for chunk in range(chunks):
        for j in range(1, group):
            give(chunk, j).wait_recv()
        give_self(chunk).wait()
        lanes = lanes_of(chunk)
        for f in range(frames):
            temporal = back[:, f, :, lanes].astype(jnp.float32)
            result[f, :, lanes] = (
                result[f, :, lanes].astype(jnp.float32)
                + temporal.reshape(patches, SIZES[chunk] * E)
            ).astype(jnp.bfloat16)
        write(chunk).start()

    for chunk in range(chunks):
        for j in range(1, group):
            exchange(chunk, peer_of(j)).wait_send()
            give(chunk, j).wait_send()
        write(chunk).wait()
    for side in range(2):
        @pl.when(chip == ends[side])
        def _():
            for z in range(chips):
                far_copy(side, z).wait_send()
    for peer in range(near):
        @pl.when(peer != my_near)
        def _():
            near_copy(peer, my_near).wait_send()


def move(source, out, sems):
    step = source.shape[2] // MOVES
    copies = [
        pltpu.make_async_copy(
            source.at[0, f, i * step : (i + 1) * step],
            out.at[0, f, i * step : (i + 1) * step],
            sems.at[f, i],
        )
        for f in range(source.shape[1])
        for i in range(MOVES)
    ]
    for copy in copies:
        copy.start()
    for copy in copies:
        copy.wait()


def solution(mesh):
    clips, group = mesh.shape["dp"], mesh.shape["frame"]

    def local(projected, codes, weight, clip_ids, frame_map, segments):
        _, _, frames, patches, width = projected.shape
        near = clips // FAR
        share = patches // group
        slots = group * frames
        rows = slots * share
        chunks = len(SIZES)
        anywhere = pl.BlockSpec(memory_space=pl.ANY)
        dma = pltpu.SemaphoreType.DMA
        bf16, f32 = jnp.bfloat16, jnp.float32
        shape = jax.ShapeDtypeStruct((1, frames, patches, width), bf16)
        mixed = pl.pallas_call(
            functools.partial(kernel, (clips, group, frames, patches, width)),
            out_shape=pltpu.VMEM(shape.shape, bf16),
            in_specs=[anywhere] * 6,
            out_specs=anywhere,
            scratch_shapes=[
                pltpu.SMEM(clip_ids.shape, clip_ids.dtype),
                pltpu.SMEM(frame_map.shape, frame_map.dtype),
                pltpu.SMEM(segments.shape, segments.dtype),
                pltpu.VMEM(codes.shape, f32),
                pltpu.VMEM(weight.shape, f32),
                pltpu.VMEM((FAR, *codes.shape[1:]), f32),
                pltpu.VMEM((near, FAR, *codes.shape[1:]), f32),
                pltpu.VMEM((slots, width), f32),
                pltpu.VMEM((rows, rows), f32),
                pltpu.VMEM((3, frames, patches, width), bf16),
                pltpu.VMEM((group, 3, frames, share, width), bf16),
                pltpu.VMEM((group, frames, share, width), bf16),
                pltpu.VMEM((group, frames, share, width), bf16),
                pltpu.VMEM((frames, patches, width), bf16),
                dma((chunks,)),
                dma((5,)),
                dma((2, group // CORES)),
                dma((2,)),
                pltpu.SemaphoreType.REGULAR,
                pltpu.SemaphoreType.REGULAR((group,)),
                pltpu.SemaphoreType.REGULAR((near,)),
                dma((near,)),
                dma((near,)),
                dma((2,)),
                dma(()),
                dma((chunks, group)),
                dma((chunks, group)),
                dma((chunks, group)),
                dma((chunks, group)),
            ],
            compiler_params=pltpu.CompilerParams(
                collective_id=0,
                has_side_effects=True,
                vmem_limit_bytes=64_000_000,
            ),
        )(
            *(
                pltpu.with_memory_space_constraint(x, pltpu.HBM)
                for x in (clip_ids, frame_map, segments, codes, weight, projected)
            )
        )
        return pl.pallas_call(
            move,
            out_shape=shape,
            in_specs=[anywhere],
            out_specs=anywhere,
            scratch_shapes=[dma((frames, MOVES))],
        )(pltpu.with_memory_space_constraint(mixed, pltpu.VMEM))

    return jax.shard_map(
        local,
        mesh=mesh,
        in_specs=(
            P(None, "dp", "frame", None, "mp"),
            P("dp", None, None),
            P(None, "mp"),
            P(),
            P(),
            P("dp", None),
        ),
        out_specs=P("dp", "frame", None, "mp"),
        check_vma=False,
    )
```

```python
import functools

import jax
import jax.numpy as jnp
from jax import lax
from jax.experimental import pallas as pl
from jax.experimental.pallas import tpu as pltpu
from jax.sharding import PartitionSpec as P

MESH = pl.DeviceIdType.MESH
E = 128
FAR = 3
CORES = 2
SIZES = (5, 3, 2)
MOVES = 4


def softmax(scores):
    peak = jnp.max(scores, axis=-1, keepdims=True)
    weights = jnp.exp(scores - peak)
    return (weights / jnp.sum(weights, axis=-1, keepdims=True)).astype(jnp.bfloat16)


def scores_of(q, k):
    return lax.dot_general(
        q, k, (((1,), (1,)), ((), ())), preferred_element_type=jnp.float32
    )


def kernel(
    sizes,
    clip_ids_in,
    frame_map_in,
    segments_in,
    codes_in,
    weight_in,
    projected,
    out,
    clip_ids,
    frame_map,
    segments,
    codes,
    weight,
    far_codes,
    all_codes,
    action,
    bias,
    own,
    got,
    done,
    back,
    small_sem,
    far_send,
    far_recv,
    far_hello,
    hello,
    near_hello,
    near_send,
    near_recv,
    code_sem,
    own_sem,
    send_sem,
    recv_sem,
    back_send,
    back_recv,
):
    clips, group, frames, patches, width = sizes
    near = clips // FAR
    share = patches // group
    slots = group * frames
    rows = slots * share
    chunks = len(SIZES)
    chips = group // CORES
    starts = [sum(SIZES[:c]) for c in range(chunks)]
    scale = 1.0 / E**0.5
    clip = lax.axis_index("dp")
    me = lax.axis_index("frame")
    mp = lax.axis_index("mp")
    my_far, my_near = clip // near, lax.rem(clip, near)
    chip, core = me // CORES, lax.rem(me, CORES)

    def peer_of(j):
        return jnp.bitwise_xor(me, j)

    def at_frame(peer):
        return (clip, peer, mp)

    def at_near(peer):
        return (my_far * near + peer, me, mp)

    def at_far(part, chip_there):
        return (part * near + my_near, chip_there * CORES + core, mp)

    ends = (chips - 1, 0)
    there = (lax.rem(my_far + 1, FAR), lax.rem(my_far + FAR - 1, FAR))

    small = [
        pltpu.make_async_copy(a, b, small_sem.at[i])
        for i, (a, b) in enumerate(
            (
                (clip_ids_in, clip_ids),
                (frame_map_in, frame_map),
                (segments_in, segments),
                (codes_in, codes),
                (weight_in, weight),
            )
        )
    ]
    own_in = pltpu.make_async_copy(projected.at[0:3, 0], own, own_sem)

    corner = (my_far == 0) & (mp == 0)
    shift = jnp.where(corner & (my_near == 0), 1, 0)
    near_shift = jnp.where(corner & (me == 0), 1, 0)

    def rank(peer):
        return lax.rem(peer + group - shift, group)

    def near_rank(peer):
        return lax.rem(peer + near - near_shift, near)

    my_rank, my_near_rank = rank(me), near_rank(my_near)

    barrier = pltpu.get_barrier_semaphore()
    for peer in range(group):
        @pl.when(rank(peer) > my_rank)
        def _():
            pl.semaphore_signal(
                barrier, inc=1, device_id=at_frame(peer), device_id_type=MESH
            )

    for peer in range(near):
        @pl.when(near_rank(peer) > my_near_rank)
        def _():
            pl.semaphore_signal(
                barrier, inc=1, device_id=at_near(peer), device_id_type=MESH
            )

    for side in range(2):
        @pl.when((chip == ends[side]) & (there[side] > my_far))
        def _():
            for z in range(chips):
                pl.semaphore_signal(
                    barrier,
                    inc=1,
                    device_id=at_far(there[side], z),
                    device_id_type=MESH,
                )

        @pl.when(there[side] > my_far)
        def _():
            pl.semaphore_signal(
                barrier,
                inc=1,
                device_id=at_far(there[side], ends[1 - side]),
                device_id_type=MESH,
            )

    for copy in small:
        copy.start()
    own_in.start()
    heard = my_rank + my_near_rank
    for side in range(2):
        earlier = there[side] < my_far
        heard = heard + jnp.where(earlier, 1, 0)
        heard = heard + jnp.where(earlier & (chip == ends[side]), chips, 0)

    @pl.when(heard > 0)
    def _():
        pl.semaphore_wait(barrier, heard)


    def lanes_of(chunk):
        return slice(starts[chunk] * E, (starts[chunk] + SIZES[chunk]) * E)

    def part(owner, chunk):
        mine = pl.ds(pl.multiple_of(owner * share, share), share)
        return projected.at[3:6, 0, :, mine, lanes_of(chunk)]

    def exchange(chunk, peer):
        return pltpu.make_async_remote_copy(
            src_ref=part(peer, chunk),
            dst_ref=got.at[me, :, :, :, lanes_of(chunk)],
            send_sem=send_sem.at[chunk, peer],
            recv_sem=recv_sem.at[chunk, me],
            device_id=at_frame(peer),
            device_id_type=MESH,
        )

    def got_from(chunk, peer):
        return pltpu.make_async_remote_copy(
            src_ref=part(peer, chunk),
            dst_ref=got.at[peer, :, :, :, lanes_of(chunk)],
            send_sem=send_sem.at[chunk, peer],
            recv_sem=recv_sem.at[chunk, peer],
            device_id=at_frame(peer),
            device_id_type=MESH,
        )

    def keep(chunk):
        return pltpu.make_async_copy(
            part(me, chunk),
            got.at[me, :, :, :, lanes_of(chunk)],
            recv_sem.at[chunk, me],
        )

    for j in range(1, group):
        @pl.when(rank(peer_of(j)) < my_rank)
        def _():
            exchange(0, peer_of(j)).start()
            pl.semaphore_signal(
                hello.at[me], inc=1, device_id=at_frame(peer_of(j)), device_id_type=MESH
            )

    for peer in (*range(1, group), 0):
        @pl.when(rank(peer) > my_rank)
        def _():
            pl.semaphore_wait(hello.at[peer], 1)
            exchange(0, peer).start()

    keep(0).start()
    for chunk in range(1, chunks):
        for j in range(1, group):
            exchange(chunk, peer_of(j)).start()
        keep(chunk).start()

    for peer in range(near):
        @pl.when(near_rank(peer) < my_near_rank)
        def _():
            pl.semaphore_signal(
                near_hello.at[my_near],
                inc=1,
                device_id=at_near(peer),
                device_id_type=MESH,
            )

    for side in range(2):
        @pl.when(there[side] < my_far)
        def _():
            pl.semaphore_signal(
                far_hello,
                inc=1,
                device_id=at_far(there[side], ends[1 - side]),
                device_id_type=MESH,
            )

    for copy in small:
        copy.wait()

    def far_copy(side, z):
        return pltpu.make_async_remote_copy(
            src_ref=codes.at[0],
            dst_ref=far_codes.at[my_far],
            send_sem=far_send.at[side, z],
            recv_sem=far_recv.at[side],
            device_id=at_far(there[side], z),
            device_id_type=MESH,
        )

    def far_start(side, when):
        @pl.when((chip == ends[side]) & when)
        def _():
            for z in range(chips):
                far_copy(side, z).start()

    for side in range(2):
        far_start(side, there[side] < my_far)
    own_code = pltpu.make_async_copy(codes.at[0], far_codes.at[my_far], code_sem.at[0])
    own_code.start()

    row = lax.broadcasted_iota(jnp.int32, (rows, rows), 0)
    column = lax.broadcasted_iota(jnp.int32, (rows, rows), 1)
    row_time = jnp.zeros((rows, 1), jnp.int32)
    row_part = jnp.zeros((rows, 1), jnp.int32)
    col_time = jnp.zeros((1, rows), jnp.int32)
    col_part = jnp.zeros((1, rows), jnp.int32)
    row_slot = lax.broadcasted_iota(jnp.int32, (rows, 1), 0) // share
    col_slot = lax.broadcasted_iota(jnp.int32, (1, rows), 1) // share
    for s in range(slots):
        time = frame_map[s]
        episode = segments[0, time]
        row_time = jnp.where(row_slot == s, time, row_time)
        row_part = jnp.where(row_slot == s, episode, row_part)
        col_time = jnp.where(col_slot == s, time, col_time)
        col_part = jnp.where(col_slot == s, episode, col_part)
    allowed = (
        (lax.rem(row, share) == lax.rem(column, share))
        & (col_time <= row_time)
        & (col_part == row_part)
    )
    bias[...] = jnp.where(allowed, 0.0, -1e30)

    own_in.wait()

    def one_head(head, carry):
        lanes = pl.ds(pl.multiple_of(head * E, E), E)
        for f in range(frames):
            probs = softmax(scores_of(own[0, f, :, lanes], own[1, f, :, lanes]) * scale)
            out[0, f, :, lanes] = jnp.dot(
                probs, own[2, f, :, lanes], preferred_element_type=jnp.float32
            ).astype(jnp.bfloat16)
        return carry

    lax.fori_loop(0, width // E, one_head, 0)

    for side in range(2):
        @pl.when((chip == ends[side]) & (there[side] > my_far))
        def _():
            pl.semaphore_wait(far_hello, chips)

        far_start(side, there[side] > my_far)
    own_code.wait()
    for side in range(2):
        pltpu.make_async_remote_copy(
            src_ref=codes.at[0],
            dst_ref=far_codes.at[there[1 - side]],
            send_sem=far_send.at[side, 0],
            recv_sem=far_recv.at[side],
            device_id=at_far(there[side], 0),
            device_id_type=MESH,
        ).wait_recv()

    def near_copy(peer, source):
        return pltpu.make_async_remote_copy(
            src_ref=far_codes,
            dst_ref=all_codes.at[source],
            send_sem=near_send.at[peer],
            recv_sem=near_recv.at[source],
            device_id=at_near(peer),
            device_id_type=MESH,
        )

    for peer in range(near):
        @pl.when(near_rank(peer) < my_near_rank)
        def _():
            near_copy(peer, my_near).start()

    for peer in (*range(1, near), 0):
        @pl.when(near_rank(peer) > my_near_rank)
        def _():
            pl.semaphore_wait(near_hello.at[peer], 1)
            near_copy(peer, my_near).start()

    near_own = pltpu.make_async_copy(far_codes, all_codes.at[my_near], code_sem.at[1])
    near_own.start()
    for peer in range(near):
        @pl.when(peer != my_near)
        def _():
            near_copy(peer, peer).wait_recv()

    near_own.wait()

    by_clip = jnp.zeros(codes.shape[1:], jnp.float32)
    for i in range(clips):
        by_clip = by_clip + jnp.where(
            clip_ids[i] == clip, all_codes[i % near, i // near], 0.0
        )
    slot_of = lax.broadcasted_iota(jnp.int32, (slots, 1), 0)
    time_of = jnp.zeros((slots, 1), jnp.int32)
    for s in range(slots):
        time_of = jnp.where(slot_of == s, frame_map[s], time_of)
    by_slot = jnp.zeros(by_clip.shape, jnp.float32)
    for t in range(slots):
        by_slot = by_slot + jnp.where(time_of == t, by_clip[t : t + 1], 0.0)
    action[...] = jnp.dot(
        by_slot,
        weight[...],
        precision=lax.Precision.HIGHEST,
        preferred_element_type=jnp.float32,
    )

    def give(chunk, j):
        peer = peer_of(j)
        return pltpu.make_async_remote_copy(
            src_ref=done.at[peer, :, :, lanes_of(chunk)],
            dst_ref=back.at[me, :, :, lanes_of(chunk)],
            send_sem=back_send.at[chunk, j],
            recv_sem=back_recv.at[chunk, j],
            device_id=at_frame(peer),
            device_id_type=MESH,
        )

    def give_self(chunk):
        return pltpu.make_async_copy(
            done.at[me, :, :, lanes_of(chunk)],
            back.at[me, :, :, lanes_of(chunk)],
            back_recv.at[chunk, 0],
        )

    def attend(head, carry):
        lanes = pl.ds(pl.multiple_of(head * E, E), E)
        q = got[:, 0, :, :, lanes].reshape(rows, E)
        k = got[:, 1, :, :, lanes].reshape(rows, E)
        raw = got[:, 2, :, :, lanes].reshape(slots, share, E)
        added = action[:, lanes]
        v = (raw.astype(jnp.float32) + added[:, None, :]).astype(jnp.bfloat16)
        probs = softmax(scores_of(q, k) * scale + bias[...])
        mixed = jnp.dot(
            probs, v.reshape(rows, E), preferred_element_type=jnp.float32
        ).astype(jnp.bfloat16)
        done[:, :, :, lanes] = mixed.reshape(group, frames, share, E)
        return carry

    for chunk in range(chunks):
        for j in range(1, group):
            got_from(chunk, peer_of(j)).wait_recv()
        keep(chunk).wait()
        lax.fori_loop(starts[chunk], starts[chunk] + SIZES[chunk], attend, 0)
        for j in range(1, group):
            give(chunk, j).start()
        give_self(chunk).start()

    for chunk in range(chunks):
        for j in range(1, group):
            give(chunk, j).wait_recv()
        give_self(chunk).wait()
        lanes = lanes_of(chunk)
        for f in range(frames):
            temporal = back[:, f, :, lanes].astype(jnp.float32)
            out[0, f, :, lanes] = (
                out[0, f, :, lanes].astype(jnp.float32)
                + temporal.reshape(patches, SIZES[chunk] * E)
            ).astype(jnp.bfloat16)

    for chunk in range(chunks):
        for j in range(1, group):
            exchange(chunk, peer_of(j)).wait_send()
            give(chunk, j).wait_send()
    for side in range(2):
        @pl.when(chip == ends[side])
        def _():
            for z in range(chips):
                far_copy(side, z).wait_send()
    for peer in range(near):
        @pl.when(peer != my_near)
        def _():
            near_copy(peer, my_near).wait_send()


def move(source, out, sems):
    step = source.shape[2] // MOVES
    copies = [
        pltpu.make_async_copy(
            source.at[0, f, i * step : (i + 1) * step],
            out.at[0, f, i * step : (i + 1) * step],
            sems.at[f, i],
        )
        for f in range(source.shape[1])
        for i in range(MOVES)
    ]
    for copy in copies:
        copy.start()
    for copy in copies:
        copy.wait()


def solution(mesh):
    clips, group = mesh.shape["dp"], mesh.shape["frame"]

    def local(projected, codes, weight, clip_ids, frame_map, segments):
        _, _, frames, patches, width = projected.shape
        near = clips // FAR
        share = patches // group
        slots = group * frames
        rows = slots * share
        chunks = len(SIZES)
        anywhere = pl.BlockSpec(memory_space=pl.ANY)
        dma = pltpu.SemaphoreType.DMA
        bf16, f32 = jnp.bfloat16, jnp.float32
        shape = jax.ShapeDtypeStruct((1, frames, patches, width), bf16)
        mixed = pl.pallas_call(
            functools.partial(kernel, (clips, group, frames, patches, width)),
            out_shape=pltpu.VMEM(shape.shape, bf16),
            in_specs=[anywhere] * 6,
            out_specs=pl.BlockSpec(memory_space=pltpu.VMEM),
            scratch_shapes=[
                pltpu.SMEM(clip_ids.shape, clip_ids.dtype),
                pltpu.SMEM(frame_map.shape, frame_map.dtype),
                pltpu.SMEM(segments.shape, segments.dtype),
                pltpu.VMEM(codes.shape, f32),
                pltpu.VMEM(weight.shape, f32),
                pltpu.VMEM((FAR, *codes.shape[1:]), f32),
                pltpu.VMEM((near, FAR, *codes.shape[1:]), f32),
                pltpu.VMEM((slots, width), f32),
                pltpu.VMEM((rows, rows), f32),
                pltpu.VMEM((3, frames, patches, width), bf16),
                pltpu.VMEM((group, 3, frames, share, width), bf16),
                pltpu.VMEM((group, frames, share, width), bf16),
                pltpu.VMEM((group, frames, share, width), bf16),
                dma((5,)),
                dma((2, group // CORES)),
                dma((2,)),
                pltpu.SemaphoreType.REGULAR,
                pltpu.SemaphoreType.REGULAR((group,)),
                pltpu.SemaphoreType.REGULAR((near,)),
                dma((near,)),
                dma((near,)),
                dma((2,)),
                dma(()),
                dma((chunks, group)),
                dma((chunks, group)),
                dma((chunks, group)),
                dma((chunks, group)),
            ],
            compiler_params=pltpu.CompilerParams(
                collective_id=0,
                has_side_effects=True,
                vmem_limit_bytes=64_000_000,
            ),
        )(
            *(
                pltpu.with_memory_space_constraint(x, pltpu.HBM)
                for x in (clip_ids, frame_map, segments, codes, weight, projected)
            )
        )
        return pl.pallas_call(
            move,
            out_shape=shape,
            in_specs=[anywhere],
            out_specs=anywhere,
            scratch_shapes=[dma((frames, MOVES))],
        )(pltpu.with_memory_space_constraint(mixed, pltpu.VMEM))

    return jax.shard_map(
        local,
        mesh=mesh,
        in_specs=(
            P(None, "dp", "frame", None, "mp"),
            P("dp", None, None),
            P(None, "mp"),
            P(),
            P(),
            P("dp", None),
        ),
        out_specs=P("dp", "frame", None, "mp"),
        check_vma=False,
    )
```

```python
import functools

import jax
import jax.numpy as jnp
from jax import lax
from jax.experimental import pallas as pl
from jax.experimental.pallas import tpu as pltpu
from jax.sharding import PartitionSpec as P

MESH = pl.DeviceIdType.MESH
E = 128
FAR = 3
CORES = 2
SIZES = (5, 3, 2)
MOVES = 4


def softmax(scores):
    peak = jnp.max(scores, axis=-1, keepdims=True)
    weights = jnp.exp(scores - peak)
    return (weights / jnp.sum(weights, axis=-1, keepdims=True)).astype(jnp.bfloat16)


def scores_of(q, k):
    return lax.dot_general(
        q, k, (((1,), (1,)), ((), ())), preferred_element_type=jnp.float32
    )


def kernel(
    sizes,
    clip_ids_in,
    frame_map_in,
    segments_in,
    codes_in,
    weight_in,
    projected,
    out,
    clip_ids,
    frame_map,
    segments,
    codes,
    weight,
    far_codes,
    all_codes,
    action,
    bias,
    own,
    got,
    done,
    back,
    small_sem,
    far_send,
    far_recv,
    far_hello,
    hello,
    near_hello,
    near_send,
    near_recv,
    code_sem,
    own_sem,
    send_sem,
    recv_sem,
    back_send,
    back_recv,
):
    clips, group, frames, patches, width = sizes
    near = clips // FAR
    share = patches // group
    slots = group * frames
    rows = slots * share
    chunks = len(SIZES)
    chips = group // CORES
    starts = [sum(SIZES[:c]) for c in range(chunks)]
    scale = 1.0 / E**0.5
    clip = lax.axis_index("dp")
    me = lax.axis_index("frame")
    mp = lax.axis_index("mp")
    my_far, my_near = clip // near, lax.rem(clip, near)
    chip, core = me // CORES, lax.rem(me, CORES)

    def peer_of(j):
        return jnp.bitwise_xor(me, j)

    def at_frame(peer):
        return (clip, peer, mp)

    def at_near(peer):
        return (my_far * near + peer, me, mp)

    def at_far(part, chip_there):
        return (part * near + my_near, chip_there * CORES + core, mp)

    ends = (chips - 1, 0)
    there = (lax.rem(my_far + 1, FAR), lax.rem(my_far + FAR - 1, FAR))

    small = [
        pltpu.make_async_copy(a, b, small_sem.at[i])
        for i, (a, b) in enumerate(
            (
                (clip_ids_in, clip_ids),
                (frame_map_in, frame_map),
                (segments_in, segments),
                (codes_in, codes),
                (weight_in, weight),
            )
        )
    ]
    own_in = pltpu.make_async_copy(projected.at[0:3, 0], own, own_sem)

    corner = (my_far == 0) & (mp == 0)
    shift = jnp.where(corner & (my_near == 0), 1, 0)
    near_shift = jnp.where(corner & (me == 0), 1, 0)

    def rank(peer):
        return lax.rem(peer + group - shift, group)

    def near_rank(peer):
        return lax.rem(peer + near - near_shift, near)

    my_rank, my_near_rank = rank(me), near_rank(my_near)

    barrier = pltpu.get_barrier_semaphore()
    for peer in range(group):
        @pl.when(rank(peer) > my_rank)
        def _():
            pl.semaphore_signal(
                barrier, inc=1, device_id=at_frame(peer), device_id_type=MESH
            )

    beside = (lax.rem(my_near + 1, near), lax.rem(my_near + near - 1, near))
    for side in range(2):
        @pl.when(near_rank(beside[side]) > my_near_rank)
        def _():
            pl.semaphore_signal(
                barrier, inc=1, device_id=at_near(beside[side]), device_id_type=MESH
            )

    for side in range(2):
        @pl.when((chip == ends[side]) & (there[side] > my_far))
        def _():
            for z in range(chips):
                pl.semaphore_signal(
                    barrier,
                    inc=1,
                    device_id=at_far(there[side], z),
                    device_id_type=MESH,
                )

        @pl.when(there[side] > my_far)
        def _():
            pl.semaphore_signal(
                barrier,
                inc=1,
                device_id=at_far(there[side], ends[1 - side]),
                device_id_type=MESH,
            )

    for copy in small:
        copy.start()
    own_in.start()
    heard = my_rank
    for side in range(2):
        heard = heard + jnp.where(near_rank(beside[side]) < my_near_rank, 1, 0)
        earlier = there[side] < my_far
        heard = heard + jnp.where(earlier, 1, 0)
        heard = heard + jnp.where(earlier & (chip == ends[side]), chips, 0)

    @pl.when(heard > 0)
    def _():
        pl.semaphore_wait(barrier, heard)


    def lanes_of(chunk):
        return slice(starts[chunk] * E, (starts[chunk] + SIZES[chunk]) * E)

    def part(owner, chunk):
        mine = pl.ds(pl.multiple_of(owner * share, share), share)
        return projected.at[3:6, 0, :, mine, lanes_of(chunk)]

    def exchange(chunk, peer):
        return pltpu.make_async_remote_copy(
            src_ref=part(peer, chunk),
            dst_ref=got.at[me, :, :, :, lanes_of(chunk)],
            send_sem=send_sem.at[chunk, peer],
            recv_sem=recv_sem.at[chunk, me],
            device_id=at_frame(peer),
            device_id_type=MESH,
        )

    def got_from(chunk, peer):
        return pltpu.make_async_remote_copy(
            src_ref=part(peer, chunk),
            dst_ref=got.at[peer, :, :, :, lanes_of(chunk)],
            send_sem=send_sem.at[chunk, peer],
            recv_sem=recv_sem.at[chunk, peer],
            device_id=at_frame(peer),
            device_id_type=MESH,
        )

    def keep(chunk):
        return pltpu.make_async_copy(
            part(me, chunk),
            got.at[me, :, :, :, lanes_of(chunk)],
            recv_sem.at[chunk, me],
        )

    for j in range(1, group):
        @pl.when(rank(peer_of(j)) < my_rank)
        def _():
            exchange(0, peer_of(j)).start()
            pl.semaphore_signal(
                hello.at[me], inc=1, device_id=at_frame(peer_of(j)), device_id_type=MESH
            )

    for peer in (*range(1, group), 0):
        @pl.when(rank(peer) > my_rank)
        def _():
            pl.semaphore_wait(hello.at[peer], 1)
            exchange(0, peer).start()

    keep(0).start()
    for chunk in range(1, chunks):
        for j in range(1, group):
            exchange(chunk, peer_of(j)).start()
        keep(chunk).start()

    for side in range(2):
        @pl.when(near_rank(beside[side]) < my_near_rank)
        def _():
            pl.semaphore_signal(
                near_hello.at[1 - side],
                inc=1,
                device_id=at_near(beside[side]),
                device_id_type=MESH,
            )

    for side in range(2):
        @pl.when(there[side] < my_far)
        def _():
            pl.semaphore_signal(
                far_hello,
                inc=1,
                device_id=at_far(there[side], ends[1 - side]),
                device_id_type=MESH,
            )

    for copy in small:
        copy.wait()

    def far_copy(side, z):
        return pltpu.make_async_remote_copy(
            src_ref=codes.at[0],
            dst_ref=far_codes.at[my_far],
            send_sem=far_send.at[side, z],
            recv_sem=far_recv.at[side],
            device_id=at_far(there[side], z),
            device_id_type=MESH,
        )

    def far_start(side, when):
        @pl.when((chip == ends[side]) & when)
        def _():
            for z in range(chips):
                far_copy(side, z).start()

    for side in range(2):
        far_start(side, there[side] < my_far)
    own_code = pltpu.make_async_copy(codes.at[0], far_codes.at[my_far], code_sem.at[0])
    own_code.start()

    row = lax.broadcasted_iota(jnp.int32, (rows, rows), 0)
    column = lax.broadcasted_iota(jnp.int32, (rows, rows), 1)
    row_time = jnp.zeros((rows, 1), jnp.int32)
    row_part = jnp.zeros((rows, 1), jnp.int32)
    col_time = jnp.zeros((1, rows), jnp.int32)
    col_part = jnp.zeros((1, rows), jnp.int32)
    row_slot = lax.broadcasted_iota(jnp.int32, (rows, 1), 0) // share
    col_slot = lax.broadcasted_iota(jnp.int32, (1, rows), 1) // share
    for s in range(slots):
        time = frame_map[s]
        episode = segments[0, time]
        row_time = jnp.where(row_slot == s, time, row_time)
        row_part = jnp.where(row_slot == s, episode, row_part)
        col_time = jnp.where(col_slot == s, time, col_time)
        col_part = jnp.where(col_slot == s, episode, col_part)
    allowed = (
        (lax.rem(row, share) == lax.rem(column, share))
        & (col_time <= row_time)
        & (col_part == row_part)
    )
    bias[...] = jnp.where(allowed, 0.0, -1e30)

    own_in.wait()

    def one_head(head, carry):
        lanes = pl.ds(pl.multiple_of(head * E, E), E)
        for f in range(frames):
            probs = softmax(scores_of(own[0, f, :, lanes], own[1, f, :, lanes]) * scale)
            out[0, f, :, lanes] = jnp.dot(
                probs, own[2, f, :, lanes], preferred_element_type=jnp.float32
            ).astype(jnp.bfloat16)
        return carry

    lax.fori_loop(0, width // E, one_head, 0)

    for side in range(2):
        @pl.when((chip == ends[side]) & (there[side] > my_far))
        def _():
            pl.semaphore_wait(far_hello, chips)

        far_start(side, there[side] > my_far)
    own_code.wait()
    for side in range(2):
        pltpu.make_async_remote_copy(
            src_ref=codes.at[0],
            dst_ref=far_codes.at[there[1 - side]],
            send_sem=far_send.at[side, 0],
            recv_sem=far_recv.at[side],
            device_id=at_far(there[side], 0),
            device_id_type=MESH,
        ).wait_recv()

    hops = (near // 2, (near - 1) // 2)

    def near_copy(side, hop):
        source = lax.rem(my_near + (near - hop if side == 0 else hop), near)
        return pltpu.make_async_remote_copy(
            src_ref=far_codes if hop == 0 else all_codes.at[source],
            dst_ref=all_codes.at[source],
            send_sem=near_send.at[side, hop],
            recv_sem=near_recv.at[side, hop],
            device_id=at_near(beside[side]),
            device_id_type=MESH,
        )

    def near_arrived(side, hop):
        source = lax.rem(my_near + (near - hop - 1 if side == 0 else hop + 1), near)
        return pltpu.make_async_remote_copy(
            src_ref=far_codes,
            dst_ref=all_codes.at[source],
            send_sem=near_send.at[side, hop],
            recv_sem=near_recv.at[side, hop],
            device_id=at_near(beside[side]),
            device_id_type=MESH,
        )

    for side in range(2):
        @pl.when(near_rank(beside[side]) > my_near_rank)
        def _():
            pl.semaphore_wait(near_hello.at[side], 1)

        near_copy(side, 0).start()
    near_own = pltpu.make_async_copy(far_codes, all_codes.at[my_near], code_sem.at[1])
    near_own.start()
    for hop in range(hops[0]):
        for side in range(2):
            if hop < hops[side]:
                near_arrived(side, hop).wait_recv()
            if hop + 1 < hops[side]:
                near_copy(side, hop + 1).start()
    near_own.wait()

    by_clip = jnp.zeros(codes.shape[1:], jnp.float32)
    for i in range(clips):
        by_clip = by_clip + jnp.where(
            clip_ids[i] == clip, all_codes[i % near, i // near], 0.0
        )
    slot_of = lax.broadcasted_iota(jnp.int32, (slots, 1), 0)
    time_of = jnp.zeros((slots, 1), jnp.int32)
    for s in range(slots):
        time_of = jnp.where(slot_of == s, frame_map[s], time_of)
    by_slot = jnp.zeros(by_clip.shape, jnp.float32)
    for t in range(slots):
        by_slot = by_slot + jnp.where(time_of == t, by_clip[t : t + 1], 0.0)
    action[...] = jnp.dot(
        by_slot,
        weight[...],
        precision=lax.Precision.HIGHEST,
        preferred_element_type=jnp.float32,
    )

    def give(chunk, j):
        peer = peer_of(j)
        return pltpu.make_async_remote_copy(
            src_ref=done.at[peer, :, :, lanes_of(chunk)],
            dst_ref=back.at[me, :, :, lanes_of(chunk)],
            send_sem=back_send.at[chunk, j],
            recv_sem=back_recv.at[chunk, j],
            device_id=at_frame(peer),
            device_id_type=MESH,
        )

    def give_self(chunk):
        return pltpu.make_async_copy(
            done.at[me, :, :, lanes_of(chunk)],
            back.at[me, :, :, lanes_of(chunk)],
            back_recv.at[chunk, 0],
        )

    def attend(head, carry):
        lanes = pl.ds(pl.multiple_of(head * E, E), E)
        q = got[:, 0, :, :, lanes].reshape(rows, E)
        k = got[:, 1, :, :, lanes].reshape(rows, E)
        raw = got[:, 2, :, :, lanes].reshape(slots, share, E)
        added = action[:, lanes]
        v = (raw.astype(jnp.float32) + added[:, None, :]).astype(jnp.bfloat16)
        probs = softmax(scores_of(q, k) * scale + bias[...])
        mixed = jnp.dot(
            probs, v.reshape(rows, E), preferred_element_type=jnp.float32
        ).astype(jnp.bfloat16)
        done[:, :, :, lanes] = mixed.reshape(group, frames, share, E)
        return carry

    for chunk in range(chunks):
        for j in range(1, group):
            got_from(chunk, peer_of(j)).wait_recv()
        keep(chunk).wait()
        lax.fori_loop(starts[chunk], starts[chunk] + SIZES[chunk], attend, 0)
        for j in range(1, group):
            give(chunk, j).start()
        give_self(chunk).start()

    for chunk in range(chunks):
        for j in range(1, group):
            give(chunk, j).wait_recv()
        give_self(chunk).wait()
        lanes = lanes_of(chunk)
        for f in range(frames):
            temporal = back[:, f, :, lanes].astype(jnp.float32)
            out[0, f, :, lanes] = (
                out[0, f, :, lanes].astype(jnp.float32)
                + temporal.reshape(patches, SIZES[chunk] * E)
            ).astype(jnp.bfloat16)

    for chunk in range(chunks):
        for j in range(1, group):
            exchange(chunk, peer_of(j)).wait_send()
            give(chunk, j).wait_send()
    for side in range(2):
        @pl.when(chip == ends[side])
        def _():
            for z in range(chips):
                far_copy(side, z).wait_send()
    for side in range(2):
        for hop in range(hops[side]):
            near_copy(side, hop).wait_send()


def move(source, out, sems):
    step = source.shape[2] // MOVES
    copies = [
        pltpu.make_async_copy(
            source.at[0, f, i * step : (i + 1) * step],
            out.at[0, f, i * step : (i + 1) * step],
            sems.at[f, i],
        )
        for f in range(source.shape[1])
        for i in range(MOVES)
    ]
    for copy in copies:
        copy.start()
    for copy in copies:
        copy.wait()


def solution(mesh):
    clips, group = mesh.shape["dp"], mesh.shape["frame"]

    def local(projected, codes, weight, clip_ids, frame_map, segments):
        _, _, frames, patches, width = projected.shape
        near = clips // FAR
        share = patches // group
        slots = group * frames
        rows = slots * share
        chunks = len(SIZES)
        anywhere = pl.BlockSpec(memory_space=pl.ANY)
        dma = pltpu.SemaphoreType.DMA
        bf16, f32 = jnp.bfloat16, jnp.float32
        shape = jax.ShapeDtypeStruct((1, frames, patches, width), bf16)
        mixed = pl.pallas_call(
            functools.partial(kernel, (clips, group, frames, patches, width)),
            out_shape=pltpu.VMEM(shape.shape, bf16),
            in_specs=[anywhere] * 6,
            out_specs=pl.BlockSpec(memory_space=pltpu.VMEM),
            scratch_shapes=[
                pltpu.SMEM(clip_ids.shape, clip_ids.dtype),
                pltpu.SMEM(frame_map.shape, frame_map.dtype),
                pltpu.SMEM(segments.shape, segments.dtype),
                pltpu.VMEM(codes.shape, f32),
                pltpu.VMEM(weight.shape, f32),
                pltpu.VMEM((FAR, *codes.shape[1:]), f32),
                pltpu.VMEM((near, FAR, *codes.shape[1:]), f32),
                pltpu.VMEM((slots, width), f32),
                pltpu.VMEM((rows, rows), f32),
                pltpu.VMEM((3, frames, patches, width), bf16),
                pltpu.VMEM((group, 3, frames, share, width), bf16),
                pltpu.VMEM((group, frames, share, width), bf16),
                pltpu.VMEM((group, frames, share, width), bf16),
                dma((5,)),
                dma((2, group // CORES)),
                dma((2,)),
                pltpu.SemaphoreType.REGULAR,
                pltpu.SemaphoreType.REGULAR((group,)),
                pltpu.SemaphoreType.REGULAR((2,)),
                dma((2, near // 2)),
                dma((2, near // 2)),
                dma((2,)),
                dma(()),
                dma((chunks, group)),
                dma((chunks, group)),
                dma((chunks, group)),
                dma((chunks, group)),
            ],
            compiler_params=pltpu.CompilerParams(
                collective_id=0,
                has_side_effects=True,
                vmem_limit_bytes=64_000_000,
            ),
        )(
            *(
                pltpu.with_memory_space_constraint(x, pltpu.HBM)
                for x in (clip_ids, frame_map, segments, codes, weight, projected)
            )
        )
        return pl.pallas_call(
            move,
            out_shape=shape,
            in_specs=[anywhere],
            out_specs=anywhere,
            scratch_shapes=[dma((frames, MOVES))],
        )(pltpu.with_memory_space_constraint(mixed, pltpu.VMEM))

    return jax.shard_map(
        local,
        mesh=mesh,
        in_specs=(
            P(None, "dp", "frame", None, "mp"),
            P("dp", None, None),
            P(None, "mp"),
            P(),
            P(),
            P("dp", None),
        ),
        out_specs=P("dp", "frame", None, "mp"),
        check_vma=False,
    )
```

```python
import functools

import jax
import jax.numpy as jnp
from jax import lax
from jax.experimental import pallas as pl
from jax.experimental.pallas import tpu as pltpu
from jax.sharding import PartitionSpec as P

MESH = pl.DeviceIdType.MESH
E = 128
FAR = 3
CORES = 2
SIZES = (5, 3, 2)
MOVES = 4


def softmax(scores):
    peak = jnp.max(scores, axis=-1, keepdims=True)
    weights = jnp.exp(scores - peak)
    return (weights / jnp.sum(weights, axis=-1, keepdims=True)).astype(jnp.bfloat16)


def scores_of(q, k):
    return lax.dot_general(
        q, k, (((1,), (1,)), ((), ())), preferred_element_type=jnp.float32
    )


def kernel(
    sizes,
    clip_ids_in,
    frame_map_in,
    segments_in,
    codes_in,
    weight_in,
    projected,
    out,
    clip_ids,
    frame_map,
    segments,
    codes,
    weight,
    far_codes,
    all_codes,
    row_out,
    row_in,
    action,
    bias,
    own,
    got,
    done,
    back,
    small_sem,
    far_send,
    far_recv,
    row_send,
    row_recv,
    far_hello,
    hello,
    near_hello,
    near_send,
    near_recv,
    code_sem,
    own_sem,
    send_sem,
    recv_sem,
    back_send,
    back_recv,
):
    clips, group, frames, patches, width = sizes
    near = clips // FAR
    share = patches // group
    slots = group * frames
    rows = slots * share
    chunks = len(SIZES)
    chips = group // CORES
    starts = [sum(SIZES[:c]) for c in range(chunks)]
    scale = 1.0 / E**0.5
    clip = lax.axis_index("dp")
    me = lax.axis_index("frame")
    mp = lax.axis_index("mp")
    my_far, my_near = clip // near, lax.rem(clip, near)
    chip, core = me // CORES, lax.rem(me, CORES)

    def peer_of(j):
        return jnp.bitwise_xor(me, j)

    def at_frame(peer):
        return (clip, peer, mp)

    def at_near(peer):
        return (my_far * near + peer, me, mp)

    def at_far(part, chip_there):
        return (part * near + my_near, chip_there * CORES + core, mp)

    ends = (chips - 1, 0)
    there = (lax.rem(my_far + 1, FAR), lax.rem(my_far + FAR - 1, FAR))

    small = [
        pltpu.make_async_copy(a, b, small_sem.at[i])
        for i, (a, b) in enumerate(
            (
                (clip_ids_in, clip_ids),
                (frame_map_in, frame_map),
                (segments_in, segments),
                (codes_in, codes),
                (weight_in, weight),
            )
        )
    ]
    own_in = pltpu.make_async_copy(projected.at[0:3, 0], own, own_sem)

    corner = (my_far == 0) & (mp == 0)
    shift = jnp.where(corner & (my_near == 0), 1, 0)
    near_shift = jnp.where(corner & (me == 0), 1, 0)

    def rank(peer):
        return lax.rem(peer + group - shift, group)

    def near_rank(peer):
        return lax.rem(peer + near - near_shift, near)

    my_rank, my_near_rank = rank(me), near_rank(my_near)

    barrier = pltpu.get_barrier_semaphore()
    for peer in range(group):
        @pl.when(rank(peer) > my_rank)
        def _():
            pl.semaphore_signal(
                barrier, inc=1, device_id=at_frame(peer), device_id_type=MESH
            )

    beside = (lax.rem(my_near + 1, near), lax.rem(my_near + near - 1, near))
    for side in range(2):
        @pl.when((chip == 0) & (near_rank(beside[side]) > my_near_rank))
        def _():
            pl.semaphore_signal(
                barrier, inc=1, device_id=at_near(beside[side]), device_id_type=MESH
            )

    reach = (1, chips)
    reached = (chip >= 0, chip == 0)
    for side in range(2):
        @pl.when((chip == ends[side]) & (there[side] > my_far))
        def _():
            for z in range(reach[side]):
                pl.semaphore_signal(
                    barrier,
                    inc=1,
                    device_id=at_far(there[side], z),
                    device_id_type=MESH,
                )

        @pl.when(reached[side] & (there[side] > my_far))
        def _():
            pl.semaphore_signal(
                barrier,
                inc=1,
                device_id=at_far(there[side], ends[1 - side]),
                device_id_type=MESH,
            )

    heard = my_rank
    for side in range(2):
        lower = near_rank(beside[side]) < my_near_rank
        heard = heard + jnp.where((chip == 0) & lower, 1, 0)
        earlier = there[side] < my_far
        heard = heard + jnp.where(earlier & reached[side], 1, 0)
        heard = heard + jnp.where(earlier & (chip == ends[side]), reach[side], 0)

    @pl.when(heard > 0)
    def _():
        pl.semaphore_wait(barrier, heard)


    def lanes_of(chunk):
        return slice(starts[chunk] * E, (starts[chunk] + SIZES[chunk]) * E)

    def part(owner, chunk):
        mine = pl.ds(pl.multiple_of(owner * share, share), share)
        return projected.at[3:6, 0, :, mine, lanes_of(chunk)]

    def exchange(chunk, peer):
        return pltpu.make_async_remote_copy(
            src_ref=part(peer, chunk),
            dst_ref=got.at[me, :, :, :, lanes_of(chunk)],
            send_sem=send_sem.at[chunk, peer],
            recv_sem=recv_sem.at[chunk, me],
            device_id=at_frame(peer),
            device_id_type=MESH,
        )

    def got_from(chunk, peer):
        return pltpu.make_async_remote_copy(
            src_ref=part(peer, chunk),
            dst_ref=got.at[peer, :, :, :, lanes_of(chunk)],
            send_sem=send_sem.at[chunk, peer],
            recv_sem=recv_sem.at[chunk, peer],
            device_id=at_frame(peer),
            device_id_type=MESH,
        )

    def keep(chunk):
        return pltpu.make_async_copy(
            part(me, chunk),
            got.at[me, :, :, :, lanes_of(chunk)],
            recv_sem.at[chunk, me],
        )

    for j in range(1, group):
        @pl.when(rank(peer_of(j)) < my_rank)
        def _():
            pl.semaphore_signal(
                hello.at[me], inc=1, device_id=at_frame(peer_of(j)), device_id_type=MESH
            )

    for j in range(1, group):
        @pl.when(rank(peer_of(j)) < my_rank)
        def _():
            exchange(0, peer_of(j)).start()

    for copy in small:
        copy.start()
    own_in.start()
    for peer in (*range(1, group), 0):
        @pl.when(rank(peer) > my_rank)
        def _():
            pl.semaphore_wait(hello.at[peer], 1)
            exchange(0, peer).start()

    keep(0).start()
    for chunk in range(1, chunks):
        for j in range(1, group):
            exchange(chunk, peer_of(j)).start()
        keep(chunk).start()

    for side in range(2):
        @pl.when((chip == 0) & (near_rank(beside[side]) < my_near_rank))
        def _():
            pl.semaphore_signal(
                near_hello.at[1 - side],
                inc=1,
                device_id=at_near(beside[side]),
                device_id_type=MESH,
            )

    for side in range(2):
        @pl.when(reached[side] & (there[side] < my_far))
        def _():
            pl.semaphore_signal(
                far_hello,
                inc=1,
                device_id=at_far(there[side], ends[1 - side]),
                device_id_type=MESH,
            )

    for copy in small:
        copy.wait()

    def far_copy(side, source):
        return pltpu.make_async_remote_copy(
            src_ref=codes.at[0],
            dst_ref=far_codes.at[source],
            send_sem=far_send.at[side],
            recv_sem=far_recv.at[side],
            device_id=at_far(there[side], 0),
            device_id_type=MESH,
        )

    def far_start(side, when):
        @pl.when((chip == ends[side]) & when)
        def _():
            far_copy(side, my_far).start()

    def row_copy(z):
        return pltpu.make_async_remote_copy(
            src_ref=row_out,
            dst_ref=row_in,
            send_sem=row_send.at[z],
            recv_sem=row_recv,
            device_id=at_far(there[1], z),
            device_id_type=MESH,
        )

    for side in range(2):
        far_start(side, there[side] < my_far)
    own_code = pltpu.make_async_copy(codes.at[0], far_codes.at[my_far], code_sem.at[0])
    own_code.start()

    row = lax.broadcasted_iota(jnp.int32, (rows, rows), 0)
    column = lax.broadcasted_iota(jnp.int32, (rows, rows), 1)
    row_time = jnp.zeros((rows, 1), jnp.int32)
    row_part = jnp.zeros((rows, 1), jnp.int32)
    col_time = jnp.zeros((1, rows), jnp.int32)
    col_part = jnp.zeros((1, rows), jnp.int32)
    row_slot = lax.broadcasted_iota(jnp.int32, (rows, 1), 0) // share
    col_slot = lax.broadcasted_iota(jnp.int32, (1, rows), 1) // share
    for s in range(slots):
        time = frame_map[s]
        episode = segments[0, time]
        row_time = jnp.where(row_slot == s, time, row_time)
        row_part = jnp.where(row_slot == s, episode, row_part)
        col_time = jnp.where(col_slot == s, time, col_time)
        col_part = jnp.where(col_slot == s, episode, col_part)
    allowed = (
        (lax.rem(row, share) == lax.rem(column, share))
        & (col_time <= row_time)
        & (col_part == row_part)
    )
    bias[...] = jnp.where(allowed, 0.0, -1e30)

    own_in.wait()

    def one_head(head, carry):
        lanes = pl.ds(pl.multiple_of(head * E, E), E)
        for f in range(frames):
            probs = softmax(scores_of(own[0, f, :, lanes], own[1, f, :, lanes]) * scale)
            out[0, f, :, lanes] = jnp.dot(
                probs, own[2, f, :, lanes], preferred_element_type=jnp.float32
            ).astype(jnp.bfloat16)
        return carry

    lax.fori_loop(0, width // E, one_head, 0)

    for side in range(2):
        @pl.when((chip == ends[side]) & (there[side] > my_far))
        def _():
            pl.semaphore_wait(far_hello, reach[side])

        far_start(side, there[side] > my_far)
    own_code.wait()

    hops = (near // 2, (near - 1) // 2)

    def near_copy(side, hop):
        source = lax.rem(my_near + (near - hop if side == 0 else hop), near)
        return pltpu.make_async_remote_copy(
            src_ref=far_codes if hop == 0 else all_codes.at[source],
            dst_ref=all_codes.at[source],
            send_sem=near_send.at[side, hop],
            recv_sem=near_recv.at[side, hop],
            device_id=at_near(beside[side]),
            device_id_type=MESH,
        )

    def near_arrived(side, hop):
        source = lax.rem(my_near + (near - hop - 1 if side == 0 else hop + 1), near)
        return pltpu.make_async_remote_copy(
            src_ref=far_codes,
            dst_ref=all_codes.at[source],
            send_sem=near_send.at[side, hop],
            recv_sem=near_recv.at[side, hop],
            device_id=at_near(beside[side]),
            device_id_type=MESH,
        )

    def row_of(wanted):
        row = jnp.zeros(codes.shape[1:], jnp.float32)
        for i in range(clips):
            row = row + jnp.where(
                clip_ids[i] == wanted, all_codes[i % near, i // near], 0.0
            )
        return row

    @pl.when(chip == 0)
    def _():
        for side in range(2):
            far_copy(side, there[1 - side]).wait_recv()
        for side in range(2):
            @pl.when(near_rank(beside[side]) > my_near_rank)
            def _():
                pl.semaphore_wait(near_hello.at[side], 1)

            near_copy(side, 0).start()
        near_own = pltpu.make_async_copy(
            far_codes, all_codes.at[my_near], code_sem.at[1]
        )
        near_own.start()
        for hop in range(hops[0]):
            for side in range(2):
                if hop < hops[side]:
                    near_arrived(side, hop).wait_recv()
                if hop + 1 < hops[side]:
                    near_copy(side, hop + 1).start()
        near_own.wait()
        row_out[...] = row_of(there[1] * near + my_near)
        row_in[...] = row_of(clip)

    @pl.when(chip > 0)
    def _():
        row_copy(1).wait_recv()

    by_clip = row_in[...]
    slot_of = lax.broadcasted_iota(jnp.int32, (slots, 1), 0)
    time_of = jnp.zeros((slots, 1), jnp.int32)
    for s in range(slots):
        time_of = jnp.where(slot_of == s, frame_map[s], time_of)
    by_slot = jnp.zeros(by_clip.shape, jnp.float32)
    for t in range(slots):
        by_slot = by_slot + jnp.where(time_of == t, by_clip[t : t + 1], 0.0)
    action[...] = jnp.dot(
        by_slot,
        weight[...],
        precision=lax.Precision.HIGHEST,
        preferred_element_type=jnp.float32,
    )

    @pl.when(chip == 0)
    def _():
        for z in range(1, chips):
            row_copy(z).start()

    def give(chunk, j):
        peer = peer_of(j)
        return pltpu.make_async_remote_copy(
            src_ref=done.at[peer, :, :, lanes_of(chunk)],
            dst_ref=back.at[me, :, :, lanes_of(chunk)],
            send_sem=back_send.at[chunk, j],
            recv_sem=back_recv.at[chunk, j],
            device_id=at_frame(peer),
            device_id_type=MESH,
        )

    def give_self(chunk):
        return pltpu.make_async_copy(
            done.at[me, :, :, lanes_of(chunk)],
            back.at[me, :, :, lanes_of(chunk)],
            back_recv.at[chunk, 0],
        )

    def attend(head, carry):
        lanes = pl.ds(pl.multiple_of(head * E, E), E)
        q = got[:, 0, :, :, lanes].reshape(rows, E)
        k = got[:, 1, :, :, lanes].reshape(rows, E)
        raw = got[:, 2, :, :, lanes].reshape(slots, share, E)
        added = action[:, lanes]
        v = (raw.astype(jnp.float32) + added[:, None, :]).astype(jnp.bfloat16)
        probs = softmax(scores_of(q, k) * scale + bias[...])
        mixed = jnp.dot(
            probs, v.reshape(rows, E), preferred_element_type=jnp.float32
        ).astype(jnp.bfloat16)
        done[:, :, :, lanes] = mixed.reshape(group, frames, share, E)
        return carry

    for chunk in range(chunks):
        for j in range(1, group):
            got_from(chunk, peer_of(j)).wait_recv()
        keep(chunk).wait()
        lax.fori_loop(starts[chunk], starts[chunk] + SIZES[chunk], attend, 0)
        for j in range(1, group):
            give(chunk, j).start()
        give_self(chunk).start()

    for chunk in range(chunks):
        for j in range(1, group):
            give(chunk, j).wait_recv()
        give_self(chunk).wait()
        lanes = lanes_of(chunk)
        for f in range(frames):
            temporal = back[:, f, :, lanes].astype(jnp.float32)
            out[0, f, :, lanes] = (
                out[0, f, :, lanes].astype(jnp.float32)
                + temporal.reshape(patches, SIZES[chunk] * E)
            ).astype(jnp.bfloat16)

    for chunk in range(chunks):
        for j in range(1, group):
            exchange(chunk, peer_of(j)).wait_send()
            give(chunk, j).wait_send()
    for side in range(2):
        @pl.when(chip == ends[side])
        def _():
            far_copy(side, my_far).wait_send()

    @pl.when(chip == 0)
    def _():
        for side in range(2):
            for hop in range(hops[side]):
                near_copy(side, hop).wait_send()
        for z in range(1, chips):
            row_copy(z).wait_send()


def move(source, out, sems):
    step = source.shape[2] // MOVES
    copies = [
        pltpu.make_async_copy(
            source.at[0, f, i * step : (i + 1) * step],
            out.at[0, f, i * step : (i + 1) * step],
            sems.at[f, i],
        )
        for f in range(source.shape[1])
        for i in range(MOVES)
    ]
    for copy in copies:
        copy.start()
    for copy in copies:
        copy.wait()


def solution(mesh):
    clips, group = mesh.shape["dp"], mesh.shape["frame"]

    def local(projected, codes, weight, clip_ids, frame_map, segments):
        _, _, frames, patches, width = projected.shape
        near = clips // FAR
        share = patches // group
        slots = group * frames
        rows = slots * share
        chunks = len(SIZES)
        anywhere = pl.BlockSpec(memory_space=pl.ANY)
        dma = pltpu.SemaphoreType.DMA
        bf16, f32 = jnp.bfloat16, jnp.float32
        shape = jax.ShapeDtypeStruct((1, frames, patches, width), bf16)
        mixed = pl.pallas_call(
            functools.partial(kernel, (clips, group, frames, patches, width)),
            out_shape=pltpu.VMEM(shape.shape, bf16),
            in_specs=[anywhere] * 6,
            out_specs=pl.BlockSpec(memory_space=pltpu.VMEM),
            scratch_shapes=[
                pltpu.SMEM(clip_ids.shape, clip_ids.dtype),
                pltpu.SMEM(frame_map.shape, frame_map.dtype),
                pltpu.SMEM(segments.shape, segments.dtype),
                pltpu.VMEM(codes.shape, f32),
                pltpu.VMEM(weight.shape, f32),
                pltpu.VMEM((FAR, *codes.shape[1:]), f32),
                pltpu.VMEM((near, FAR, *codes.shape[1:]), f32),
                pltpu.VMEM(codes.shape[1:], f32),
                pltpu.VMEM(codes.shape[1:], f32),
                pltpu.VMEM((slots, width), f32),
                pltpu.VMEM((rows, rows), f32),
                pltpu.VMEM((3, frames, patches, width), bf16),
                pltpu.VMEM((group, 3, frames, share, width), bf16),
                pltpu.VMEM((group, frames, share, width), bf16),
                pltpu.VMEM((group, frames, share, width), bf16),
                dma((5,)),
                dma((2,)),
                dma((2,)),
                dma((group // CORES,)),
                dma(()),
                pltpu.SemaphoreType.REGULAR,
                pltpu.SemaphoreType.REGULAR((group,)),
                pltpu.SemaphoreType.REGULAR((2,)),
                dma((2, near // 2)),
                dma((2, near // 2)),
                dma((2,)),
                dma(()),
                dma((chunks, group)),
                dma((chunks, group)),
                dma((chunks, group)),
                dma((chunks, group)),
            ],
            compiler_params=pltpu.CompilerParams(
                collective_id=0,
                has_side_effects=True,
                vmem_limit_bytes=64_000_000,
            ),
        )(
            *(
                pltpu.with_memory_space_constraint(x, pltpu.HBM)
                for x in (clip_ids, frame_map, segments, codes, weight, projected)
            )
        )
        return pl.pallas_call(
            move,
            out_shape=shape,
            in_specs=[anywhere],
            out_specs=anywhere,
            scratch_shapes=[dma((frames, MOVES))],
        )(pltpu.with_memory_space_constraint(mixed, pltpu.VMEM))

    return jax.shard_map(
        local,
        mesh=mesh,
        in_specs=(
            P(None, "dp", "frame", None, "mp"),
            P("dp", None, None),
            P(None, "mp"),
            P(),
            P(),
            P("dp", None),
        ),
        out_specs=P("dp", "frame", None, "mp"),
        check_vma=False,
    )
```

```python
import functools

import jax
import jax.numpy as jnp
from jax import lax
from jax.experimental import pallas as pl
from jax.experimental.pallas import tpu as pltpu
from jax.sharding import PartitionSpec as P

MESH = pl.DeviceIdType.MESH
E = 128
FAR = 3
CORES = 2
SIZES = (4, 4, 2)
MOVES = 4


def softmax(scores):
    peak = jnp.max(scores, axis=-1, keepdims=True)
    weights = jnp.exp(scores - peak)
    return (weights / jnp.sum(weights, axis=-1, keepdims=True)).astype(jnp.bfloat16)


def scores_of(q, k):
    return lax.dot_general(
        q, k, (((1,), (1,)), ((), ())), preferred_element_type=jnp.float32
    )


def kernel(
    sizes,
    clip_ids_in,
    frame_map_in,
    segments_in,
    codes_in,
    weight_in,
    projected,
    out,
    clip_ids,
    frame_map,
    segments,
    codes,
    weight,
    far_codes,
    all_codes,
    row_out,
    row_in,
    action,
    bias,
    own,
    got,
    done,
    back,
    small_sem,
    far_send,
    far_recv,
    row_send,
    row_recv,
    far_hello,
    hello,
    near_hello,
    near_send,
    near_recv,
    code_sem,
    own_sem,
    send_sem,
    recv_sem,
    back_send,
    back_recv,
):
    clips, group, frames, patches, width = sizes
    near = clips // FAR
    share = patches // group
    slots = group * frames
    rows = slots * share
    chunks = len(SIZES)
    chips = group // CORES
    starts = [sum(SIZES[:c]) for c in range(chunks)]
    scale = 1.0 / E**0.5
    clip = lax.axis_index("dp")
    me = lax.axis_index("frame")
    mp = lax.axis_index("mp")
    my_far, my_near = clip // near, lax.rem(clip, near)
    chip, core = me // CORES, lax.rem(me, CORES)

    def peer_of(j):
        return jnp.bitwise_xor(me, j)

    def at_frame(peer):
        return (clip, peer, mp)

    def at_near(peer):
        return (my_far * near + peer, me, mp)

    def at_far(part, chip_there):
        return (part * near + my_near, chip_there * CORES + core, mp)

    ends = (chips - 1, 0)
    there = (lax.rem(my_far + 1, FAR), lax.rem(my_far + FAR - 1, FAR))

    small = [
        pltpu.make_async_copy(a, b, small_sem.at[i])
        for i, (a, b) in enumerate(
            (
                (clip_ids_in, clip_ids),
                (frame_map_in, frame_map),
                (segments_in, segments),
                (codes_in, codes),
                (weight_in, weight),
            )
        )
    ]
    own_in = pltpu.make_async_copy(projected.at[0:3, 0], own, own_sem)

    corner = (my_far == 0) & (mp == 0)
    shift = jnp.where(corner & (my_near == 0), 1, 0)
    near_shift = jnp.where(corner & (me == 0), 1, 0)

    def rank(peer):
        return lax.rem(peer + group - shift, group)

    def near_rank(peer):
        return lax.rem(peer + near - near_shift, near)

    my_rank, my_near_rank = rank(me), near_rank(my_near)

    barrier = pltpu.get_barrier_semaphore()
    for peer in range(group):
        @pl.when(rank(peer) > my_rank)
        def _():
            pl.semaphore_signal(
                barrier, inc=1, device_id=at_frame(peer), device_id_type=MESH
            )

    beside = (lax.rem(my_near + 1, near), lax.rem(my_near + near - 1, near))
    for side in range(2):
        @pl.when((chip == 0) & (near_rank(beside[side]) > my_near_rank))
        def _():
            pl.semaphore_signal(
                barrier, inc=1, device_id=at_near(beside[side]), device_id_type=MESH
            )

    reach = (1, chips)
    reached = (chip >= 0, chip == 0)
    for side in range(2):
        @pl.when((chip == ends[side]) & (there[side] > my_far))
        def _():
            for z in range(reach[side]):
                pl.semaphore_signal(
                    barrier,
                    inc=1,
                    device_id=at_far(there[side], z),
                    device_id_type=MESH,
                )

        @pl.when(reached[side] & (there[side] > my_far))
        def _():
            pl.semaphore_signal(
                barrier,
                inc=1,
                device_id=at_far(there[side], ends[1 - side]),
                device_id_type=MESH,
            )

    heard = my_rank
    for side in range(2):
        lower = near_rank(beside[side]) < my_near_rank
        heard = heard + jnp.where((chip == 0) & lower, 1, 0)
        earlier = there[side] < my_far
        heard = heard + jnp.where(earlier & reached[side], 1, 0)
        heard = heard + jnp.where(earlier & (chip == ends[side]), reach[side], 0)

    @pl.when(heard > 0)
    def _():
        pl.semaphore_wait(barrier, heard)


    def lanes_of(chunk):
        return slice(starts[chunk] * E, (starts[chunk] + SIZES[chunk]) * E)

    def part(owner, chunk):
        mine = pl.ds(pl.multiple_of(owner * share, share), share)
        return projected.at[3:6, 0, :, mine, lanes_of(chunk)]

    def exchange(chunk, peer):
        return pltpu.make_async_remote_copy(
            src_ref=part(peer, chunk),
            dst_ref=got.at[me, :, :, :, lanes_of(chunk)],
            send_sem=send_sem.at[chunk, peer],
            recv_sem=recv_sem.at[chunk, me],
            device_id=at_frame(peer),
            device_id_type=MESH,
        )

    def got_from(chunk, peer):
        return pltpu.make_async_remote_copy(
            src_ref=part(peer, chunk),
            dst_ref=got.at[peer, :, :, :, lanes_of(chunk)],
            send_sem=send_sem.at[chunk, peer],
            recv_sem=recv_sem.at[chunk, peer],
            device_id=at_frame(peer),
            device_id_type=MESH,
        )

    def keep(chunk):
        return pltpu.make_async_copy(
            part(me, chunk),
            got.at[me, :, :, :, lanes_of(chunk)],
            recv_sem.at[chunk, me],
        )

    for j in range(1, group):
        @pl.when(rank(peer_of(j)) < my_rank)
        def _():
            pl.semaphore_signal(
                hello.at[me], inc=1, device_id=at_frame(peer_of(j)), device_id_type=MESH
            )

    for j in range(1, group):
        @pl.when(rank(peer_of(j)) < my_rank)
        def _():
            exchange(0, peer_of(j)).start()

    for copy in small:
        copy.start()
    own_in.start()
    for peer in (*range(1, group), 0):
        @pl.when(rank(peer) > my_rank)
        def _():
            pl.semaphore_wait(hello.at[peer], 1)
            exchange(0, peer).start()

    keep(0).start()
    for chunk in range(1, chunks):
        for j in range(1, group):
            exchange(chunk, peer_of(j)).start()
        keep(chunk).start()

    for side in range(2):
        @pl.when((chip == 0) & (near_rank(beside[side]) < my_near_rank))
        def _():
            pl.semaphore_signal(
                near_hello.at[1 - side],
                inc=1,
                device_id=at_near(beside[side]),
                device_id_type=MESH,
            )

    for side in range(2):
        @pl.when(reached[side] & (there[side] < my_far))
        def _():
            pl.semaphore_signal(
                far_hello,
                inc=1,
                device_id=at_far(there[side], ends[1 - side]),
                device_id_type=MESH,
            )

    for copy in small:
        copy.wait()

    def far_copy(side, source):
        return pltpu.make_async_remote_copy(
            src_ref=codes.at[0],
            dst_ref=far_codes.at[source],
            send_sem=far_send.at[side],
            recv_sem=far_recv.at[side],
            device_id=at_far(there[side], 0),
            device_id_type=MESH,
        )

    def far_start(side, when):
        @pl.when((chip == ends[side]) & when)
        def _():
            far_copy(side, my_far).start()

    def row_copy(z):
        return pltpu.make_async_remote_copy(
            src_ref=row_out,
            dst_ref=row_in,
            send_sem=row_send.at[z],
            recv_sem=row_recv,
            device_id=at_far(there[1], z),
            device_id_type=MESH,
        )

    for side in range(2):
        far_start(side, there[side] < my_far)
    own_code = pltpu.make_async_copy(codes.at[0], far_codes.at[my_far], code_sem.at[0])
    own_code.start()

    row = lax.broadcasted_iota(jnp.int32, (rows, rows), 0)
    column = lax.broadcasted_iota(jnp.int32, (rows, rows), 1)
    row_time = jnp.zeros((rows, 1), jnp.int32)
    row_part = jnp.zeros((rows, 1), jnp.int32)
    col_time = jnp.zeros((1, rows), jnp.int32)
    col_part = jnp.zeros((1, rows), jnp.int32)
    row_slot = lax.broadcasted_iota(jnp.int32, (rows, 1), 0) // share
    col_slot = lax.broadcasted_iota(jnp.int32, (1, rows), 1) // share
    for s in range(slots):
        time = frame_map[s]
        episode = segments[0, time]
        row_time = jnp.where(row_slot == s, time, row_time)
        row_part = jnp.where(row_slot == s, episode, row_part)
        col_time = jnp.where(col_slot == s, time, col_time)
        col_part = jnp.where(col_slot == s, episode, col_part)
    allowed = (
        (lax.rem(row, share) == lax.rem(column, share))
        & (col_time <= row_time)
        & (col_part == row_part)
    )
    bias[...] = jnp.where(allowed, 0.0, -1e30)

    own_in.wait()

    def one_head(head, carry):
        lanes = pl.ds(pl.multiple_of(head * E, E), E)
        for f in range(frames):
            probs = softmax(scores_of(own[0, f, :, lanes], own[1, f, :, lanes]) * scale)
            out[0, f, :, lanes] = jnp.dot(
                probs, own[2, f, :, lanes], preferred_element_type=jnp.float32
            ).astype(jnp.bfloat16)
        return carry

    lax.fori_loop(0, width // E, one_head, 0)

    for side in range(2):
        @pl.when((chip == ends[side]) & (there[side] > my_far))
        def _():
            pl.semaphore_wait(far_hello, reach[side])

        far_start(side, there[side] > my_far)
    own_code.wait()

    hops = (near // 2, (near - 1) // 2)

    def near_copy(side, hop):
        source = lax.rem(my_near + (near - hop if side == 0 else hop), near)
        return pltpu.make_async_remote_copy(
            src_ref=far_codes if hop == 0 else all_codes.at[source],
            dst_ref=all_codes.at[source],
            send_sem=near_send.at[side, hop],
            recv_sem=near_recv.at[side, hop],
            device_id=at_near(beside[side]),
            device_id_type=MESH,
        )

    def near_arrived(side, hop):
        source = lax.rem(my_near + (near - hop - 1 if side == 0 else hop + 1), near)
        return pltpu.make_async_remote_copy(
            src_ref=far_codes,
            dst_ref=all_codes.at[source],
            send_sem=near_send.at[side, hop],
            recv_sem=near_recv.at[side, hop],
            device_id=at_near(beside[side]),
            device_id_type=MESH,
        )

    def row_of(wanted):
        row = jnp.zeros(codes.shape[1:], jnp.float32)
        for i in range(clips):
            row = row + jnp.where(
                clip_ids[i] == wanted, all_codes[i % near, i // near], 0.0
            )
        return row

    @pl.when(chip == 0)
    def _():
        for side in range(2):
            far_copy(side, there[1 - side]).wait_recv()
        for side in range(2):
            @pl.when(near_rank(beside[side]) > my_near_rank)
            def _():
                pl.semaphore_wait(near_hello.at[side], 1)

            near_copy(side, 0).start()
        near_own = pltpu.make_async_copy(
            far_codes, all_codes.at[my_near], code_sem.at[1]
        )
        near_own.start()
        for hop in range(hops[0]):
            for side in range(2):
                if hop < hops[side]:
                    near_arrived(side, hop).wait_recv()
                if hop + 1 < hops[side]:
                    near_copy(side, hop + 1).start()
        near_own.wait()
        row_out[...] = row_of(there[1] * near + my_near)
        row_in[...] = row_of(clip)

    @pl.when(chip > 0)
    def _():
        row_copy(1).wait_recv()

    by_clip = row_in[...]
    slot_of = lax.broadcasted_iota(jnp.int32, (slots, 1), 0)
    time_of = jnp.zeros((slots, 1), jnp.int32)
    for s in range(slots):
        time_of = jnp.where(slot_of == s, frame_map[s], time_of)
    by_slot = jnp.zeros(by_clip.shape, jnp.float32)
    for t in range(slots):
        by_slot = by_slot + jnp.where(time_of == t, by_clip[t : t + 1], 0.0)
    action[...] = jnp.dot(
        by_slot,
        weight[...],
        precision=lax.Precision.HIGHEST,
        preferred_element_type=jnp.float32,
    )

    @pl.when(chip == 0)
    def _():
        for z in range(1, chips):
            row_copy(z).start()

    def give(chunk, j):
        peer = peer_of(j)
        return pltpu.make_async_remote_copy(
            src_ref=done.at[peer, :, :, lanes_of(chunk)],
            dst_ref=back.at[me, :, :, lanes_of(chunk)],
            send_sem=back_send.at[chunk, j],
            recv_sem=back_recv.at[chunk, j],
            device_id=at_frame(peer),
            device_id_type=MESH,
        )

    def held(j):
        return (chip == chips // 2) & (peer_of(j) // CORES == chips // 2 - 1)

    def give_self(chunk):
        return pltpu.make_async_copy(
            done.at[me, :, :, lanes_of(chunk)],
            back.at[me, :, :, lanes_of(chunk)],
            back_recv.at[chunk, 0],
        )

    def attend(head, carry):
        lanes = pl.ds(pl.multiple_of(head * E, E), E)
        q = got[:, 0, :, :, lanes].reshape(rows, E)
        k = got[:, 1, :, :, lanes].reshape(rows, E)
        raw = got[:, 2, :, :, lanes].reshape(slots, share, E)
        added = action[:, lanes]
        v = (raw.astype(jnp.float32) + added[:, None, :]).astype(jnp.bfloat16)
        probs = softmax(scores_of(q, k) * scale + bias[...])
        mixed = jnp.dot(
            probs, v.reshape(rows, E), preferred_element_type=jnp.float32
        ).astype(jnp.bfloat16)
        done[:, :, :, lanes] = mixed.reshape(group, frames, share, E)
        return carry

    for chunk in range(chunks):
        for j in range(1, group):
            got_from(chunk, peer_of(j)).wait_recv()
        keep(chunk).wait()
        lax.fori_loop(starts[chunk], starts[chunk] + SIZES[chunk], attend, 0)
        for j in range(1, group):
            if chunk == chunks - 2:
                @pl.when(jnp.logical_not(held(j)))
                def _():
                    give(chunk, j).start()
            else:
                give(chunk, j).start()
        give_self(chunk).start()
        if chunk == chunks - 1:
            for j in range(1, group):
                @pl.when(held(j))
                def _():
                    give(chunk - 1, j).start()


    for chunk in range(chunks):
        for j in range(1, group):
            give(chunk, j).wait_recv()
        give_self(chunk).wait()
        lanes = lanes_of(chunk)
        for f in range(frames):
            temporal = back[:, f, :, lanes].astype(jnp.float32)
            out[0, f, :, lanes] = (
                out[0, f, :, lanes].astype(jnp.float32)
                + temporal.reshape(patches, SIZES[chunk] * E)
            ).astype(jnp.bfloat16)

    for chunk in range(chunks):
        for j in range(1, group):
            exchange(chunk, peer_of(j)).wait_send()
            give(chunk, j).wait_send()
    for side in range(2):
        @pl.when(chip == ends[side])
        def _():
            far_copy(side, my_far).wait_send()

    @pl.when(chip == 0)
    def _():
        for side in range(2):
            for hop in range(hops[side]):
                near_copy(side, hop).wait_send()
        for z in range(1, chips):
            row_copy(z).wait_send()


def move(source, out, sems):
    step = source.shape[2] // MOVES
    copies = [
        pltpu.make_async_copy(
            source.at[0, f, i * step : (i + 1) * step],
            out.at[0, f, i * step : (i + 1) * step],
            sems.at[f, i],
        )
        for f in range(source.shape[1])
        for i in range(MOVES)
    ]
    for copy in copies:
        copy.start()
    for copy in copies:
        copy.wait()


def solution(mesh):
    clips, group = mesh.shape["dp"], mesh.shape["frame"]

    def local(projected, codes, weight, clip_ids, frame_map, segments):
        _, _, frames, patches, width = projected.shape
        near = clips // FAR
        share = patches // group
        slots = group * frames
        rows = slots * share
        chunks = len(SIZES)
        anywhere = pl.BlockSpec(memory_space=pl.ANY)
        dma = pltpu.SemaphoreType.DMA
        bf16, f32 = jnp.bfloat16, jnp.float32
        shape = jax.ShapeDtypeStruct((1, frames, patches, width), bf16)
        mixed = pl.pallas_call(
            functools.partial(kernel, (clips, group, frames, patches, width)),
            out_shape=pltpu.VMEM(shape.shape, bf16),
            in_specs=[anywhere] * 6,
            out_specs=pl.BlockSpec(memory_space=pltpu.VMEM),
            scratch_shapes=[
                pltpu.SMEM(clip_ids.shape, clip_ids.dtype),
                pltpu.SMEM(frame_map.shape, frame_map.dtype),
                pltpu.SMEM(segments.shape, segments.dtype),
                pltpu.VMEM(codes.shape, f32),
                pltpu.VMEM(weight.shape, f32),
                pltpu.VMEM((FAR, *codes.shape[1:]), f32),
                pltpu.VMEM((near, FAR, *codes.shape[1:]), f32),
                pltpu.VMEM(codes.shape[1:], f32),
                pltpu.VMEM(codes.shape[1:], f32),
                pltpu.VMEM((slots, width), f32),
                pltpu.VMEM((rows, rows), f32),
                pltpu.VMEM((3, frames, patches, width), bf16),
                pltpu.VMEM((group, 3, frames, share, width), bf16),
                pltpu.VMEM((group, frames, share, width), bf16),
                pltpu.VMEM((group, frames, share, width), bf16),
                dma((5,)),
                dma((2,)),
                dma((2,)),
                dma((group // CORES,)),
                dma(()),
                pltpu.SemaphoreType.REGULAR,
                pltpu.SemaphoreType.REGULAR((group,)),
                pltpu.SemaphoreType.REGULAR((2,)),
                dma((2, near // 2)),
                dma((2, near // 2)),
                dma((2,)),
                dma(()),
                dma((chunks, group)),
                dma((chunks, group)),
                dma((chunks, group)),
                dma((chunks, group)),
            ],
            compiler_params=pltpu.CompilerParams(
                collective_id=0,
                has_side_effects=True,
                vmem_limit_bytes=64_000_000,
            ),
        )(
            *(
                pltpu.with_memory_space_constraint(x, pltpu.HBM)
                for x in (clip_ids, frame_map, segments, codes, weight, projected)
            )
        )
        return pl.pallas_call(
            move,
            out_shape=shape,
            in_specs=[anywhere],
            out_specs=anywhere,
            scratch_shapes=[dma((frames, MOVES))],
        )(pltpu.with_memory_space_constraint(mixed, pltpu.VMEM))

    return jax.shard_map(
        local,
        mesh=mesh,
        in_specs=(
            P(None, "dp", "frame", None, "mp"),
            P("dp", None, None),
            P(None, "mp"),
            P(),
            P(),
            P("dp", None),
        ),
        out_specs=P("dp", "frame", None, "mp"),
        check_vma=False,
    )
```

```python
import functools

import jax
import jax.numpy as jnp
from jax import lax
from jax.experimental import pallas as pl
from jax.experimental.pallas import tpu as pltpu
from jax.sharding import PartitionSpec as P

MESH = pl.DeviceIdType.MESH
E = 128
FAR = 3
CORES = 2
SIZES = (3, 4, 3)
MOVES = 4


def softmax(scores):
    peak = jnp.max(scores, axis=-1, keepdims=True)
    weights = jnp.exp(scores - peak)
    return (weights / jnp.sum(weights, axis=-1, keepdims=True)).astype(jnp.bfloat16)


def scores_of(q, k):
    return lax.dot_general(
        q, k, (((1,), (1,)), ((), ())), preferred_element_type=jnp.float32
    )


def kernel(
    sizes,
    clip_ids_in,
    frame_map_in,
    segments_in,
    codes_in,
    weight_in,
    projected,
    out,
    clip_ids,
    frame_map,
    segments,
    codes,
    weight,
    far_codes,
    all_codes,
    row_out,
    row_in,
    action,
    bias,
    own,
    got,
    done,
    back,
    small_sem,
    far_send,
    far_recv,
    row_send,
    row_recv,
    far_hello,
    hello,
    near_hello,
    near_send,
    near_recv,
    code_sem,
    own_sem,
    send_sem,
    recv_sem,
    back_send,
    back_recv,
):
    clips, group, frames, patches, width = sizes
    near = clips // FAR
    share = patches // group
    slots = group * frames
    rows = slots * share
    chunks = len(SIZES)
    chips = group // CORES
    starts = [sum(SIZES[:c]) for c in range(chunks)]
    scale = 1.0 / E**0.5
    clip = lax.axis_index("dp")
    me = lax.axis_index("frame")
    mp = lax.axis_index("mp")
    my_far, my_near = clip // near, lax.rem(clip, near)
    chip, core = me // CORES, lax.rem(me, CORES)

    def peer_of(j):
        return jnp.bitwise_xor(me, j)

    def at_frame(peer):
        return (clip, peer, mp)

    def at_near(peer):
        return (my_far * near + peer, me, mp)

    def at_far(part, chip_there):
        return (part * near + my_near, chip_there * CORES + core, mp)

    ends = (chips - 1, 0)
    there = (lax.rem(my_far + 1, FAR), lax.rem(my_far + FAR - 1, FAR))

    small = [
        pltpu.make_async_copy(a, b, small_sem.at[i])
        for i, (a, b) in enumerate(
            (
                (clip_ids_in, clip_ids),
                (frame_map_in, frame_map),
                (segments_in, segments),
                (codes_in, codes),
                (weight_in, weight),
            )
        )
    ]
    own_in = pltpu.make_async_copy(projected.at[0:3, 0], own, own_sem)

    corner = (my_far == 0) & (mp == 0)
    shift = jnp.where(corner & (my_near == 0), 1, 0)
    near_shift = jnp.where(corner & (me == 0), 1, 0)

    def rank(peer):
        return lax.rem(peer + group - shift, group)

    def near_rank(peer):
        return lax.rem(peer + near - near_shift, near)

    my_rank, my_near_rank = rank(me), near_rank(my_near)

    barrier = pltpu.get_barrier_semaphore()
    for peer in range(group):
        @pl.when(rank(peer) > my_rank)
        def _():
            pl.semaphore_signal(
                barrier, inc=1, device_id=at_frame(peer), device_id_type=MESH
            )

    beside = (lax.rem(my_near + 1, near), lax.rem(my_near + near - 1, near))
    for side in range(2):
        @pl.when((chip == 0) & (near_rank(beside[side]) > my_near_rank))
        def _():
            pl.semaphore_signal(
                barrier, inc=1, device_id=at_near(beside[side]), device_id_type=MESH
            )

    reach = (1, chips)
    reached = (chip >= 0, chip == 0)
    for side in range(2):
        @pl.when((chip == ends[side]) & (there[side] > my_far))
        def _():
            for z in range(reach[side]):
                pl.semaphore_signal(
                    barrier,
                    inc=1,
                    device_id=at_far(there[side], z),
                    device_id_type=MESH,
                )

        @pl.when(reached[side] & (there[side] > my_far))
        def _():
            pl.semaphore_signal(
                barrier,
                inc=1,
                device_id=at_far(there[side], ends[1 - side]),
                device_id_type=MESH,
            )

    heard = my_rank
    for side in range(2):
        lower = near_rank(beside[side]) < my_near_rank
        heard = heard + jnp.where((chip == 0) & lower, 1, 0)
        earlier = there[side] < my_far
        heard = heard + jnp.where(earlier & reached[side], 1, 0)
        heard = heard + jnp.where(earlier & (chip == ends[side]), reach[side], 0)

    @pl.when(heard > 0)
    def _():
        pl.semaphore_wait(barrier, heard)


    def lanes_of(chunk):
        return slice(starts[chunk] * E, (starts[chunk] + SIZES[chunk]) * E)

    def part(owner, chunk):
        mine = pl.ds(pl.multiple_of(owner * share, share), share)
        return projected.at[3:6, 0, :, mine, lanes_of(chunk)]

    def exchange(chunk, peer):
        return pltpu.make_async_remote_copy(
            src_ref=part(peer, chunk),
            dst_ref=got.at[me, :, :, :, lanes_of(chunk)],
            send_sem=send_sem.at[chunk, peer],
            recv_sem=recv_sem.at[chunk, me],
            device_id=at_frame(peer),
            device_id_type=MESH,
        )

    def got_from(chunk, peer):
        return pltpu.make_async_remote_copy(
            src_ref=part(peer, chunk),
            dst_ref=got.at[peer, :, :, :, lanes_of(chunk)],
            send_sem=send_sem.at[chunk, peer],
            recv_sem=recv_sem.at[chunk, peer],
            device_id=at_frame(peer),
            device_id_type=MESH,
        )

    def keep(chunk):
        return pltpu.make_async_copy(
            part(me, chunk),
            got.at[me, :, :, :, lanes_of(chunk)],
            recv_sem.at[chunk, me],
        )

    for j in range(1, group):
        @pl.when(rank(peer_of(j)) < my_rank)
        def _():
            pl.semaphore_signal(
                hello.at[me], inc=1, device_id=at_frame(peer_of(j)), device_id_type=MESH
            )

    for j in range(1, group):
        @pl.when(rank(peer_of(j)) < my_rank)
        def _():
            exchange(0, peer_of(j)).start()

    for copy in small:
        copy.start()
    own_in.start()
    for peer in (*range(1, group), 0):
        @pl.when(rank(peer) > my_rank)
        def _():
            pl.semaphore_wait(hello.at[peer], 1)
            exchange(0, peer).start()

    keep(0).start()
    for chunk in range(1, chunks):
        for j in range(1, group):
            exchange(chunk, peer_of(j)).start()
        keep(chunk).start()

    for side in range(2):
        @pl.when((chip == 0) & (near_rank(beside[side]) < my_near_rank))
        def _():
            pl.semaphore_signal(
                near_hello.at[1 - side],
                inc=1,
                device_id=at_near(beside[side]),
                device_id_type=MESH,
            )

    for side in range(2):
        @pl.when(reached[side] & (there[side] < my_far))
        def _():
            pl.semaphore_signal(
                far_hello,
                inc=1,
                device_id=at_far(there[side], ends[1 - side]),
                device_id_type=MESH,
            )

    for copy in small:
        copy.wait()

    def far_copy(side, source):
        return pltpu.make_async_remote_copy(
            src_ref=codes.at[0],
            dst_ref=far_codes.at[source],
            send_sem=far_send.at[side],
            recv_sem=far_recv.at[side],
            device_id=at_far(there[side], 0),
            device_id_type=MESH,
        )

    def far_start(side, when):
        @pl.when((chip == ends[side]) & when)
        def _():
            far_copy(side, my_far).start()

    def row_copy(z):
        return pltpu.make_async_remote_copy(
            src_ref=row_out,
            dst_ref=row_in,
            send_sem=row_send.at[z],
            recv_sem=row_recv,
            device_id=at_far(there[1], z),
            device_id_type=MESH,
        )

    for side in range(2):
        far_start(side, there[side] < my_far)
    own_code = pltpu.make_async_copy(codes.at[0], far_codes.at[my_far], code_sem.at[0])
    own_code.start()

    row = lax.broadcasted_iota(jnp.int32, (rows, rows), 0)
    column = lax.broadcasted_iota(jnp.int32, (rows, rows), 1)
    row_time = jnp.zeros((rows, 1), jnp.int32)
    row_part = jnp.zeros((rows, 1), jnp.int32)
    col_time = jnp.zeros((1, rows), jnp.int32)
    col_part = jnp.zeros((1, rows), jnp.int32)
    row_slot = lax.broadcasted_iota(jnp.int32, (rows, 1), 0) // share
    col_slot = lax.broadcasted_iota(jnp.int32, (1, rows), 1) // share
    for s in range(slots):
        time = frame_map[s]
        episode = segments[0, time]
        row_time = jnp.where(row_slot == s, time, row_time)
        row_part = jnp.where(row_slot == s, episode, row_part)
        col_time = jnp.where(col_slot == s, time, col_time)
        col_part = jnp.where(col_slot == s, episode, col_part)
    allowed = (
        (lax.rem(row, share) == lax.rem(column, share))
        & (col_time <= row_time)
        & (col_part == row_part)
    )
    bias[...] = jnp.where(allowed, 0.0, -1e30)

    own_in.wait()

    def one_head(head, carry):
        lanes = pl.ds(pl.multiple_of(head * E, E), E)
        for f in range(frames):
            probs = softmax(scores_of(own[0, f, :, lanes], own[1, f, :, lanes]) * scale)
            out[0, f, :, lanes] = jnp.dot(
                probs, own[2, f, :, lanes], preferred_element_type=jnp.float32
            ).astype(jnp.bfloat16)
        return carry

    lax.fori_loop(0, width // E, one_head, 0)

    for side in range(2):
        @pl.when((chip == ends[side]) & (there[side] > my_far))
        def _():
            pl.semaphore_wait(far_hello, reach[side])

        far_start(side, there[side] > my_far)
    own_code.wait()

    hops = (near // 2, (near - 1) // 2)

    def near_copy(side, hop):
        source = lax.rem(my_near + (near - hop if side == 0 else hop), near)
        return pltpu.make_async_remote_copy(
            src_ref=far_codes if hop == 0 else all_codes.at[source],
            dst_ref=all_codes.at[source],
            send_sem=near_send.at[side, hop],
            recv_sem=near_recv.at[side, hop],
            device_id=at_near(beside[side]),
            device_id_type=MESH,
        )

    def near_arrived(side, hop):
        source = lax.rem(my_near + (near - hop - 1 if side == 0 else hop + 1), near)
        return pltpu.make_async_remote_copy(
            src_ref=far_codes,
            dst_ref=all_codes.at[source],
            send_sem=near_send.at[side, hop],
            recv_sem=near_recv.at[side, hop],
            device_id=at_near(beside[side]),
            device_id_type=MESH,
        )

    def row_of(wanted):
        row = jnp.zeros(codes.shape[1:], jnp.float32)
        for i in range(clips):
            row = row + jnp.where(
                clip_ids[i] == wanted, all_codes[i % near, i // near], 0.0
            )
        return row

    @pl.when(chip == 0)
    def _():
        for side in range(2):
            far_copy(side, there[1 - side]).wait_recv()
        for side in range(2):
            @pl.when(near_rank(beside[side]) > my_near_rank)
            def _():
                pl.semaphore_wait(near_hello.at[side], 1)

            near_copy(side, 0).start()
        near_own = pltpu.make_async_copy(
            far_codes, all_codes.at[my_near], code_sem.at[1]
        )
        near_own.start()
        for hop in range(hops[0]):
            for side in range(2):
                if hop < hops[side]:
                    near_arrived(side, hop).wait_recv()
                if hop + 1 < hops[side]:
                    near_copy(side, hop + 1).start()
        near_own.wait()
        row_out[...] = row_of(there[1] * near + my_near)
        row_in[...] = row_of(clip)

    @pl.when(chip > 0)
    def _():
        row_copy(1).wait_recv()

    by_clip = row_in[...]
    slot_of = lax.broadcasted_iota(jnp.int32, (slots, 1), 0)
    time_of = jnp.zeros((slots, 1), jnp.int32)
    for s in range(slots):
        time_of = jnp.where(slot_of == s, frame_map[s], time_of)
    by_slot = jnp.zeros(by_clip.shape, jnp.float32)
    for t in range(slots):
        by_slot = by_slot + jnp.where(time_of == t, by_clip[t : t + 1], 0.0)
    action[...] = jnp.dot(
        by_slot,
        weight[...],
        precision=lax.Precision.HIGHEST,
        preferred_element_type=jnp.float32,
    )

    @pl.when(chip == 0)
    def _():
        for z in range(1, chips):
            row_copy(z).start()

    def give(chunk, j):
        peer = peer_of(j)
        return pltpu.make_async_remote_copy(
            src_ref=done.at[peer, :, :, lanes_of(chunk)],
            dst_ref=back.at[me, :, :, lanes_of(chunk)],
            send_sem=back_send.at[chunk, j],
            recv_sem=back_recv.at[chunk, j],
            device_id=at_frame(peer),
            device_id_type=MESH,
        )

    def held(j):
        return (chip == chips // 2) & (peer_of(j) // CORES == chips // 2 - 1)

    def give_self(chunk):
        return pltpu.make_async_copy(
            done.at[me, :, :, lanes_of(chunk)],
            back.at[me, :, :, lanes_of(chunk)],
            back_recv.at[chunk, 0],
        )

    def attend(head, carry):
        lanes = pl.ds(pl.multiple_of(head * E, E), E)
        q = got[:, 0, :, :, lanes].reshape(rows, E)
        k = got[:, 1, :, :, lanes].reshape(rows, E)
        raw = got[:, 2, :, :, lanes].reshape(slots, share, E)
        added = action[:, lanes]
        v = (raw.astype(jnp.float32) + added[:, None, :]).astype(jnp.bfloat16)
        probs = softmax(scores_of(q, k) * scale + bias[...])
        mixed = jnp.dot(
            probs, v.reshape(rows, E), preferred_element_type=jnp.float32
        ).astype(jnp.bfloat16)
        done[:, :, :, lanes] = mixed.reshape(group, frames, share, E)
        return carry

    for chunk in range(chunks):
        for j in range(1, group):
            got_from(chunk, peer_of(j)).wait_recv()
        keep(chunk).wait()
        lax.fori_loop(starts[chunk], starts[chunk] + SIZES[chunk], attend, 0)
        for j in range(1, group):
            if chunk == chunks - 2:
                @pl.when(jnp.logical_not(held(j)))
                def _():
                    give(chunk, j).start()
            else:
                give(chunk, j).start()
        give_self(chunk).start()
        if chunk == chunks - 1:
            for j in range(1, group):
                @pl.when(held(j))
                def _():
                    give(chunk - 1, j).start()


    for chunk in range(chunks):
        for j in range(1, group):
            give(chunk, j).wait_recv()
        give_self(chunk).wait()
        lanes = lanes_of(chunk)
        for f in range(frames):
            temporal = back[:, f, :, lanes].astype(jnp.float32)
            out[0, f, :, lanes] = (
                out[0, f, :, lanes].astype(jnp.float32)
                + temporal.reshape(patches, SIZES[chunk] * E)
            ).astype(jnp.bfloat16)

    for chunk in range(chunks):
        for j in range(1, group):
            exchange(chunk, peer_of(j)).wait_send()
            give(chunk, j).wait_send()
    for side in range(2):
        @pl.when(chip == ends[side])
        def _():
            far_copy(side, my_far).wait_send()

    @pl.when(chip == 0)
    def _():
        for side in range(2):
            for hop in range(hops[side]):
                near_copy(side, hop).wait_send()
        for z in range(1, chips):
            row_copy(z).wait_send()


def move(source, out, sems):
    step = source.shape[2] // MOVES
    copies = [
        pltpu.make_async_copy(
            source.at[0, f, i * step : (i + 1) * step],
            out.at[0, f, i * step : (i + 1) * step],
            sems.at[f, i],
        )
        for f in range(source.shape[1])
        for i in range(MOVES)
    ]
    for copy in copies:
        copy.start()
    for copy in copies:
        copy.wait()


def solution(mesh):
    clips, group = mesh.shape["dp"], mesh.shape["frame"]

    def local(projected, codes, weight, clip_ids, frame_map, segments):
        _, _, frames, patches, width = projected.shape
        near = clips // FAR
        share = patches // group
        slots = group * frames
        rows = slots * share
        chunks = len(SIZES)
        anywhere = pl.BlockSpec(memory_space=pl.ANY)
        dma = pltpu.SemaphoreType.DMA
        bf16, f32 = jnp.bfloat16, jnp.float32
        shape = jax.ShapeDtypeStruct((1, frames, patches, width), bf16)
        mixed = pl.pallas_call(
            functools.partial(kernel, (clips, group, frames, patches, width)),
            out_shape=pltpu.VMEM(shape.shape, bf16),
            in_specs=[anywhere] * 6,
            out_specs=pl.BlockSpec(memory_space=pltpu.VMEM),
            scratch_shapes=[
                pltpu.SMEM(clip_ids.shape, clip_ids.dtype),
                pltpu.SMEM(frame_map.shape, frame_map.dtype),
                pltpu.SMEM(segments.shape, segments.dtype),
                pltpu.VMEM(codes.shape, f32),
                pltpu.VMEM(weight.shape, f32),
                pltpu.VMEM((FAR, *codes.shape[1:]), f32),
                pltpu.VMEM((near, FAR, *codes.shape[1:]), f32),
                pltpu.VMEM(codes.shape[1:], f32),
                pltpu.VMEM(codes.shape[1:], f32),
                pltpu.VMEM((slots, width), f32),
                pltpu.VMEM((rows, rows), f32),
                pltpu.VMEM((3, frames, patches, width), bf16),
                pltpu.VMEM((group, 3, frames, share, width), bf16),
                pltpu.VMEM((group, frames, share, width), bf16),
                pltpu.VMEM((group, frames, share, width), bf16),
                dma((5,)),
                dma((2,)),
                dma((2,)),
                dma((group // CORES,)),
                dma(()),
                pltpu.SemaphoreType.REGULAR,
                pltpu.SemaphoreType.REGULAR((group,)),
                pltpu.SemaphoreType.REGULAR((2,)),
                dma((2, near // 2)),
                dma((2, near // 2)),
                dma((2,)),
                dma(()),
                dma((chunks, group)),
                dma((chunks, group)),
                dma((chunks, group)),
                dma((chunks, group)),
            ],
            compiler_params=pltpu.CompilerParams(
                collective_id=0,
                has_side_effects=True,
                vmem_limit_bytes=64_000_000,
            ),
        )(
            *(
                pltpu.with_memory_space_constraint(x, pltpu.HBM)
                for x in (clip_ids, frame_map, segments, codes, weight, projected)
            )
        )
        return pl.pallas_call(
            move,
            out_shape=shape,
            in_specs=[anywhere],
            out_specs=anywhere,
            scratch_shapes=[dma((frames, MOVES))],
        )(pltpu.with_memory_space_constraint(mixed, pltpu.VMEM))

    return jax.shard_map(
        local,
        mesh=mesh,
        in_specs=(
            P(None, "dp", "frame", None, "mp"),
            P("dp", None, None),
            P(None, "mp"),
            P(),
            P(),
            P("dp", None),
        ),
        out_specs=P("dp", "frame", None, "mp"),
        check_vma=False,
    )
```

```python
import functools

import jax
import jax.numpy as jnp
from jax import lax
from jax.experimental import pallas as pl
from jax.experimental.pallas import tpu as pltpu
from jax.sharding import PartitionSpec as P

MESH = pl.DeviceIdType.MESH
E = 128
FAR = 3
CORES = 2
SIZES = (4, 4, 2)
MOVES = 4


def softmax(scores):
    peak = jnp.max(scores, axis=-1, keepdims=True)
    weights = jnp.exp(scores - peak)
    return (weights / jnp.sum(weights, axis=-1, keepdims=True)).astype(jnp.bfloat16)


def scores_of(q, k):
    return lax.dot_general(
        q, k, (((1,), (1,)), ((), ())), preferred_element_type=jnp.float32
    )


def kernel(
    sizes,
    clip_ids_in,
    frame_map_in,
    segments_in,
    codes_in,
    weight_in,
    projected,
    out,
    clip_ids,
    frame_map,
    segments,
    codes,
    weight,
    far_codes,
    all_codes,
    row_out,
    row_in,
    action,
    bias,
    own,
    got,
    done,
    back,
    small_sem,
    far_send,
    far_recv,
    row_send,
    row_recv,
    far_hello,
    hello,
    near_hello,
    near_send,
    near_recv,
    code_sem,
    own_sem,
    send_sem,
    recv_sem,
    back_send,
    back_recv,
):
    clips, group, frames, patches, width = sizes
    near = clips // FAR
    share = patches // group
    slots = group * frames
    rows = slots * share
    chunks = len(SIZES)
    chips = group // CORES
    starts = [sum(SIZES[:c]) for c in range(chunks)]
    scale = 1.0 / E**0.5
    clip = lax.axis_index("dp")
    me = lax.axis_index("frame")
    mp = lax.axis_index("mp")
    my_far, my_near = clip // near, lax.rem(clip, near)
    chip, core = me // CORES, lax.rem(me, CORES)

    def peer_of(j):
        return jnp.bitwise_xor(me, j)

    def at_frame(peer):
        return (clip, peer, mp)

    def at_near(peer):
        return (my_far * near + peer, me, mp)

    def at_far(part, chip_there):
        return (part * near + my_near, chip_there * CORES + core, mp)

    ends = (chips - 1, 0)
    there = (lax.rem(my_far + 1, FAR), lax.rem(my_far + FAR - 1, FAR))

    small = [
        pltpu.make_async_copy(a, b, small_sem.at[i])
        for i, (a, b) in enumerate(
            (
                (clip_ids_in, clip_ids),
                (frame_map_in, frame_map),
                (segments_in, segments),
                (codes_in, codes),
                (weight_in, weight),
            )
        )
    ]
    own_in = pltpu.make_async_copy(projected.at[0:3, 0], own, own_sem)

    corner = (my_far == 0) & (mp == 0)
    shift = jnp.where(corner & (my_near == 0), 1, 0)
    near_shift = jnp.where(corner & (me == 0), 1, 0)

    def rank(peer):
        return lax.rem(peer + group - shift, group)

    def near_rank(peer):
        return lax.rem(peer + near - near_shift, near)

    my_rank, my_near_rank = rank(me), near_rank(my_near)

    barrier = pltpu.get_barrier_semaphore()
    for peer in range(group):
        @pl.when(rank(peer) > my_rank)
        def _():
            pl.semaphore_signal(
                barrier, inc=1, device_id=at_frame(peer), device_id_type=MESH
            )

    beside = (lax.rem(my_near + 1, near), lax.rem(my_near + near - 1, near))
    for side in range(2):
        @pl.when((chip == 0) & (near_rank(beside[side]) > my_near_rank))
        def _():
            pl.semaphore_signal(
                barrier, inc=1, device_id=at_near(beside[side]), device_id_type=MESH
            )

    reach = (1, chips)
    reached = (chip >= 0, chip == 0)
    for side in range(2):
        @pl.when((chip == ends[side]) & (there[side] > my_far))
        def _():
            for z in range(reach[side]):
                pl.semaphore_signal(
                    barrier,
                    inc=1,
                    device_id=at_far(there[side], z),
                    device_id_type=MESH,
                )

        @pl.when(reached[side] & (there[side] > my_far))
        def _():
            pl.semaphore_signal(
                barrier,
                inc=1,
                device_id=at_far(there[side], ends[1 - side]),
                device_id_type=MESH,
            )

    heard = my_rank
    for side in range(2):
        lower = near_rank(beside[side]) < my_near_rank
        heard = heard + jnp.where((chip == 0) & lower, 1, 0)
        earlier = there[side] < my_far
        heard = heard + jnp.where(earlier & reached[side], 1, 0)
        heard = heard + jnp.where(earlier & (chip == ends[side]), reach[side], 0)

    @pl.when(heard > 0)
    def _():
        pl.semaphore_wait(barrier, heard)


    def lanes_of(chunk):
        return slice(starts[chunk] * E, (starts[chunk] + SIZES[chunk]) * E)

    def part(owner, chunk):
        mine = pl.ds(pl.multiple_of(owner * share, share), share)
        return projected.at[3:6, 0, :, mine, lanes_of(chunk)]

    def exchange(chunk, peer):
        return pltpu.make_async_remote_copy(
            src_ref=part(peer, chunk),
            dst_ref=got.at[me, :, :, :, lanes_of(chunk)],
            send_sem=send_sem.at[chunk, peer],
            recv_sem=recv_sem.at[chunk, me],
            device_id=at_frame(peer),
            device_id_type=MESH,
        )

    def got_from(chunk, peer):
        return pltpu.make_async_remote_copy(
            src_ref=part(peer, chunk),
            dst_ref=got.at[peer, :, :, :, lanes_of(chunk)],
            send_sem=send_sem.at[chunk, peer],
            recv_sem=recv_sem.at[chunk, peer],
            device_id=at_frame(peer),
            device_id_type=MESH,
        )

    def keep(chunk):
        return pltpu.make_async_copy(
            part(me, chunk),
            got.at[me, :, :, :, lanes_of(chunk)],
            recv_sem.at[chunk, me],
        )

    for j in range(1, group):
        @pl.when(rank(peer_of(j)) < my_rank)
        def _():
            pl.semaphore_signal(
                hello.at[me], inc=1, device_id=at_frame(peer_of(j)), device_id_type=MESH
            )

    for j in range(1, group):
        @pl.when(rank(peer_of(j)) < my_rank)
        def _():
            exchange(0, peer_of(j)).start()

    for copy in small:
        copy.start()
    own_in.start()
    for peer in (*range(1, group), 0):
        @pl.when(rank(peer) > my_rank)
        def _():
            pl.semaphore_wait(hello.at[peer], 1)
            exchange(0, peer).start()

    keep(0).start()
    for chunk in range(1, chunks):
        for j in range(1, group):
            exchange(chunk, peer_of(j)).start()
        keep(chunk).start()

    for side in range(2):
        @pl.when((chip == 0) & (near_rank(beside[side]) < my_near_rank))
        def _():
            pl.semaphore_signal(
                near_hello.at[1 - side],
                inc=1,
                device_id=at_near(beside[side]),
                device_id_type=MESH,
            )

    for side in range(2):
        @pl.when(reached[side] & (there[side] < my_far))
        def _():
            pl.semaphore_signal(
                far_hello,
                inc=1,
                device_id=at_far(there[side], ends[1 - side]),
                device_id_type=MESH,
            )

    for copy in small:
        copy.wait()

    def far_copy(side, source):
        return pltpu.make_async_remote_copy(
            src_ref=codes.at[0],
            dst_ref=far_codes.at[source],
            send_sem=far_send.at[side],
            recv_sem=far_recv.at[side],
            device_id=at_far(there[side], 0),
            device_id_type=MESH,
        )

    def far_start(side, when):
        @pl.when((chip == ends[side]) & when)
        def _():
            far_copy(side, my_far).start()

    def row_copy(z):
        return pltpu.make_async_remote_copy(
            src_ref=row_out,
            dst_ref=row_in,
            send_sem=row_send.at[z],
            recv_sem=row_recv,
            device_id=at_far(there[1], z),
            device_id_type=MESH,
        )

    for side in range(2):
        far_start(side, there[side] < my_far)
    own_code = pltpu.make_async_copy(codes.at[0], far_codes.at[my_far], code_sem.at[0])
    own_code.start()

    row = lax.broadcasted_iota(jnp.int32, (rows, rows), 0)
    column = lax.broadcasted_iota(jnp.int32, (rows, rows), 1)
    row_time = jnp.zeros((rows, 1), jnp.int32)
    row_part = jnp.zeros((rows, 1), jnp.int32)
    col_time = jnp.zeros((1, rows), jnp.int32)
    col_part = jnp.zeros((1, rows), jnp.int32)
    row_slot = lax.broadcasted_iota(jnp.int32, (rows, 1), 0) // share
    col_slot = lax.broadcasted_iota(jnp.int32, (1, rows), 1) // share
    for s in range(slots):
        time = frame_map[s]
        episode = segments[0, time]
        row_time = jnp.where(row_slot == s, time, row_time)
        row_part = jnp.where(row_slot == s, episode, row_part)
        col_time = jnp.where(col_slot == s, time, col_time)
        col_part = jnp.where(col_slot == s, episode, col_part)
    allowed = (
        (lax.rem(row, share) == lax.rem(column, share))
        & (col_time <= row_time)
        & (col_part == row_part)
    )
    bias[...] = jnp.where(allowed, 0.0, -1e30)

    own_in.wait()

    def one_head(head, carry):
        lanes = pl.ds(pl.multiple_of(head * E, E), E)
        for f in range(frames):
            probs = softmax(scores_of(own[0, f, :, lanes], own[1, f, :, lanes]) * scale)
            out[0, f, :, lanes] = jnp.dot(
                probs, own[2, f, :, lanes], preferred_element_type=jnp.float32
            ).astype(jnp.bfloat16)
        return carry

    lax.fori_loop(0, width // E, one_head, 0)

    for side in range(2):
        @pl.when((chip == ends[side]) & (there[side] > my_far))
        def _():
            pl.semaphore_wait(far_hello, reach[side])

        far_start(side, there[side] > my_far)
    own_code.wait()

    hops = (near // 2, (near - 1) // 2)

    def near_copy(side, hop):
        source = lax.rem(my_near + (near - hop if side == 0 else hop), near)
        return pltpu.make_async_remote_copy(
            src_ref=far_codes if hop == 0 else all_codes.at[source],
            dst_ref=all_codes.at[source],
            send_sem=near_send.at[side, hop],
            recv_sem=near_recv.at[side, hop],
            device_id=at_near(beside[side]),
            device_id_type=MESH,
        )

    def near_arrived(side, hop):
        source = lax.rem(my_near + (near - hop - 1 if side == 0 else hop + 1), near)
        return pltpu.make_async_remote_copy(
            src_ref=far_codes,
            dst_ref=all_codes.at[source],
            send_sem=near_send.at[side, hop],
            recv_sem=near_recv.at[side, hop],
            device_id=at_near(beside[side]),
            device_id_type=MESH,
        )

    def row_of(wanted):
        row = jnp.zeros(codes.shape[1:], jnp.float32)
        for i in range(clips):
            row = row + jnp.where(
                clip_ids[i] == wanted, all_codes[i % near, i // near], 0.0
            )
        return row

    @pl.when(chip == 0)
    def _():
        for side in range(2):
            far_copy(side, there[1 - side]).wait_recv()
        for side in range(2):
            @pl.when(near_rank(beside[side]) > my_near_rank)
            def _():
                pl.semaphore_wait(near_hello.at[side], 1)

            near_copy(side, 0).start()
        near_own = pltpu.make_async_copy(
            far_codes, all_codes.at[my_near], code_sem.at[1]
        )
        near_own.start()
        for hop in range(hops[0]):
            for side in range(2):
                if hop < hops[side]:
                    near_arrived(side, hop).wait_recv()
                if hop + 1 < hops[side]:
                    near_copy(side, hop + 1).start()
        near_own.wait()
        row_out[...] = row_of(there[1] * near + my_near)
        row_in[...] = row_of(clip)

    @pl.when(chip > 0)
    def _():
        row_copy(1).wait_recv()

    by_clip = row_in[...]
    slot_of = lax.broadcasted_iota(jnp.int32, (slots, 1), 0)
    time_of = jnp.zeros((slots, 1), jnp.int32)
    for s in range(slots):
        time_of = jnp.where(slot_of == s, frame_map[s], time_of)
    by_slot = jnp.zeros(by_clip.shape, jnp.float32)
    for t in range(slots):
        by_slot = by_slot + jnp.where(time_of == t, by_clip[t : t + 1], 0.0)
    action[...] = jnp.dot(
        by_slot,
        weight[...],
        precision=lax.Precision.HIGHEST,
        preferred_element_type=jnp.float32,
    )

    @pl.when(chip == 0)
    def _():
        for z in range(1, chips):
            row_copy(z).start()

    def give(chunk, j):
        peer = peer_of(j)
        return pltpu.make_async_remote_copy(
            src_ref=done.at[peer, :, :, lanes_of(chunk)],
            dst_ref=back.at[me, :, :, lanes_of(chunk)],
            send_sem=back_send.at[chunk, j],
            recv_sem=back_recv.at[chunk, j],
            device_id=at_frame(peer),
            device_id_type=MESH,
        )

    def held(j):
        return (chip >= chips // 2) & (peer_of(j) // CORES == chips // 2 - 1)

    def give_self(chunk):
        return pltpu.make_async_copy(
            done.at[me, :, :, lanes_of(chunk)],
            back.at[me, :, :, lanes_of(chunk)],
            back_recv.at[chunk, 0],
        )

    def attend(head, carry):
        lanes = pl.ds(pl.multiple_of(head * E, E), E)
        q = got[:, 0, :, :, lanes].reshape(rows, E)
        k = got[:, 1, :, :, lanes].reshape(rows, E)
        raw = got[:, 2, :, :, lanes].reshape(slots, share, E)
        added = action[:, lanes]
        v = (raw.astype(jnp.float32) + added[:, None, :]).astype(jnp.bfloat16)
        probs = softmax(scores_of(q, k) * scale + bias[...])
        mixed = jnp.dot(
            probs, v.reshape(rows, E), preferred_element_type=jnp.float32
        ).astype(jnp.bfloat16)
        done[:, :, :, lanes] = mixed.reshape(group, frames, share, E)
        return carry

    for chunk in range(chunks):
        for j in range(1, group):
            got_from(chunk, peer_of(j)).wait_recv()
        keep(chunk).wait()
        lax.fori_loop(starts[chunk], starts[chunk] + SIZES[chunk], attend, 0)
        for j in range(1, group):
            if chunk == chunks - 2:
                @pl.when(jnp.logical_not(held(j)))
                def _():
                    give(chunk, j).start()
            else:
                give(chunk, j).start()
        give_self(chunk).start()
        if chunk == chunks - 1:
            for j in range(1, group):
                @pl.when(held(j))
                def _():
                    give(chunk - 1, j).start()


    for chunk in range(chunks):
        for j in range(1, group):
            give(chunk, j).wait_recv()
        give_self(chunk).wait()
        lanes = lanes_of(chunk)
        for f in range(frames):
            temporal = back[:, f, :, lanes].astype(jnp.float32)
            out[0, f, :, lanes] = (
                out[0, f, :, lanes].astype(jnp.float32)
                + temporal.reshape(patches, SIZES[chunk] * E)
            ).astype(jnp.bfloat16)

    for chunk in range(chunks):
        for j in range(1, group):
            exchange(chunk, peer_of(j)).wait_send()
            give(chunk, j).wait_send()
    for side in range(2):
        @pl.when(chip == ends[side])
        def _():
            far_copy(side, my_far).wait_send()

    @pl.when(chip == 0)
    def _():
        for side in range(2):
            for hop in range(hops[side]):
                near_copy(side, hop).wait_send()
        for z in range(1, chips):
            row_copy(z).wait_send()


def move(source, out, sems):
    step = source.shape[2] // MOVES
    copies = [
        pltpu.make_async_copy(
            source.at[0, f, i * step : (i + 1) * step],
            out.at[0, f, i * step : (i + 1) * step],
            sems.at[f, i],
        )
        for f in range(source.shape[1])
        for i in range(MOVES)
    ]
    for copy in copies:
        copy.start()
    for copy in copies:
        copy.wait()


def solution(mesh):
    clips, group = mesh.shape["dp"], mesh.shape["frame"]

    def local(projected, codes, weight, clip_ids, frame_map, segments):
        _, _, frames, patches, width = projected.shape
        near = clips // FAR
        share = patches // group
        slots = group * frames
        rows = slots * share
        chunks = len(SIZES)
        anywhere = pl.BlockSpec(memory_space=pl.ANY)
        dma = pltpu.SemaphoreType.DMA
        bf16, f32 = jnp.bfloat16, jnp.float32
        shape = jax.ShapeDtypeStruct((1, frames, patches, width), bf16)
        mixed = pl.pallas_call(
            functools.partial(kernel, (clips, group, frames, patches, width)),
            out_shape=pltpu.VMEM(shape.shape, bf16),
            in_specs=[anywhere] * 6,
            out_specs=pl.BlockSpec(memory_space=pltpu.VMEM),
            scratch_shapes=[
                pltpu.SMEM(clip_ids.shape, clip_ids.dtype),
                pltpu.SMEM(frame_map.shape, frame_map.dtype),
                pltpu.SMEM(segments.shape, segments.dtype),
                pltpu.VMEM(codes.shape, f32),
                pltpu.VMEM(weight.shape, f32),
                pltpu.VMEM((FAR, *codes.shape[1:]), f32),
                pltpu.VMEM((near, FAR, *codes.shape[1:]), f32),
                pltpu.VMEM(codes.shape[1:], f32),
                pltpu.VMEM(codes.shape[1:], f32),
                pltpu.VMEM((slots, width), f32),
                pltpu.VMEM((rows, rows), f32),
                pltpu.VMEM((3, frames, patches, width), bf16),
                pltpu.VMEM((group, 3, frames, share, width), bf16),
                pltpu.VMEM((group, frames, share, width), bf16),
                pltpu.VMEM((group, frames, share, width), bf16),
                dma((5,)),
                dma((2,)),
                dma((2,)),
                dma((group // CORES,)),
                dma(()),
                pltpu.SemaphoreType.REGULAR,
                pltpu.SemaphoreType.REGULAR((group,)),
                pltpu.SemaphoreType.REGULAR((2,)),
                dma((2, near // 2)),
                dma((2, near // 2)),
                dma((2,)),
                dma(()),
                dma((chunks, group)),
                dma((chunks, group)),
                dma((chunks, group)),
                dma((chunks, group)),
            ],
            compiler_params=pltpu.CompilerParams(
                collective_id=0,
                has_side_effects=True,
                vmem_limit_bytes=64_000_000,
            ),
        )(
            *(
                pltpu.with_memory_space_constraint(x, pltpu.HBM)
                for x in (clip_ids, frame_map, segments, codes, weight, projected)
            )
        )
        return pl.pallas_call(
            move,
            out_shape=shape,
            in_specs=[anywhere],
            out_specs=anywhere,
            scratch_shapes=[dma((frames, MOVES))],
        )(pltpu.with_memory_space_constraint(mixed, pltpu.VMEM))

    return jax.shard_map(
        local,
        mesh=mesh,
        in_specs=(
            P(None, "dp", "frame", None, "mp"),
            P("dp", None, None),
            P(None, "mp"),
            P(),
            P(),
            P("dp", None),
        ),
        out_specs=P("dp", "frame", None, "mp"),
        check_vma=False,
    )
```
